32 devices in a mesh: fsdp: 16 (over z, x, core), dp: 2 (over y).
Axes of the slice: x: 2, y: 2, z: 4, core: 2. Of those that a mesh axis runs over, the one named last changes fastest.
Arguments:
- tokens: bfloat16 [24576, 1024], P(('fsdp', 'dp')), may hold values from -6 to 6
- cotangent: bfloat16 [24576, 1024], P(('fsdp', 'dp')), may hold values from -6 to 6
- segments: int32 [24576], replicated, may hold values from 0 to 47, never falling along the last dimension, each value on 1 to 577 neighbouring positions
- adapter_ids: int32 [48], replicated, may hold values from 0 to 7
- ln1_gain: float32 [1024], replicated, may hold values from 0.5 to 1.5
- ln1_bias: float32 [1024], replicated, may hold values from -1.5 to 1.5
- w_query: bfloat16 [1024, 1024], P(('fsdp', 'dp')), may hold values from -0.1875 to 0.1875
- b_query: float32 [1024], replicated, may hold values from -2.5 to 2.5
- w_key: bfloat16 [1024, 1024], P(('fsdp', 'dp')), may hold values from -0.1875 to 0.1875
- w_value: bfloat16 [1024, 1024], P(('fsdp', 'dp')), may hold values from -0.1875 to 0.1875
- b_value: float32 [1024], replicated, may hold values from -2.5 to 2.5
- w_out: bfloat16 [1024, 1024], P(('fsdp', 'dp')), may hold values from -4 to 4
- b_out: float32 [1024], replicated, may hold values from -2.5 to 2.5
- ln2_gain: float32 [1024], replicated, may hold values from 0.5 to 1.5
- ln2_bias: float32 [1024], replicated, may hold values from -1.5 to 1.5
- w_up: bfloat16 [1024, 4096], P(('fsdp', 'dp')), may hold values from -0.1875 to 0.1875
- b_up: float32 [4096], replicated, may hold values from -2.5 to 2.5
- w_down: bfloat16 [4096, 1024], P(('fsdp', 'dp')), may hold values from -0.1875 to 0.1875
- b_down: float32 [1024], replicated, may hold values from -2.5 to 2.5
- query_in: bfloat16 [1024, 128], P(('fsdp', 'dp')), may hold values from -0.1875 to 0.1875
- query_out: bfloat16 [1024, 128], P(('fsdp', 'dp')), may hold values from -0.75 to 0.75
- value_in: bfloat16 [1024, 128], P(('fsdp', 'dp')), may hold values from -0.1875 to 0.1875
- value_out: bfloat16 [1024, 128], P(('fsdp', 'dp')), may hold values from -0.75 to 0.75
- up_in: bfloat16 [1024, 128], P(('fsdp', 'dp')), may hold values from -0.1875 to 0.1875
- up_out: bfloat16 [4096, 128], P(('fsdp', 'dp')), may hold values from -0.75 to 0.75
- down_in: bfloat16 [4096, 128], P(('fsdp', 'dp')), may hold values from -0.1875 to 0.1875
- down_out: bfloat16 [1024, 128], P(('fsdp', 'dp')), may hold values from -0.75 to 0.75
Outputs:
- block_out: bfloat16 [24576, 1024], P(('fsdp', 'dp'))
- grad_input: bfloat16 [24576, 1024], P(('fsdp', 'dp'))
- grad_query_in: float32 [1024, 128], P(('fsdp', 'dp'))
- grad_query_out: float32 [1024, 128], P(('fsdp', 'dp'))
- grad_value_in: float32 [1024, 128], P(('fsdp', 'dp'))
- grad_value_out: float32 [1024, 128], P(('fsdp', 'dp'))
- grad_up_in: float32 [1024, 128], P(('fsdp', 'dp'))
- grad_up_out: float32 [4096, 128], P(('fsdp', 'dp'))
- grad_down_in: float32 [4096, 128], P(('fsdp', 'dp'))
- grad_down_out: float32 [1024, 128], P(('fsdp', 'dp'))
The draws below stay inside these ranges and needn't reach their ends.
Inputs may be any that keep to these rules, and one draw needn't show every extreme that they name: `segments`: image numbers never fall along the packed order; each image holds 1 to 577 consecutive tokens, and one holds exactly 577.
All inputs are finite; a program needn't handle non-finite values.
Results may differ from the reference program's by a relative error of at most 0.014.
Values may be sent and summed in bfloat16 or wider, within the bound.
No kernel may reach another device: no remote copies, remote signals or barrier semaphores. Data moves between devices by JAX's collectives and lax.ppermute only.
A program may use at most 384 MiB of HBM per device.

```python
import math
import jax
import jax.numpy as jnp
import numpy as np
from jax import lax

D = 1024
HEADS = 16
FF = 4096
IMG_LEN = 577
HALO = 576
RANK = 16
ADAPTERS = 8
AR = 128
TOK_DEV = 768
IMG_MEAN = 512
TOKENS = 24576
IMAGES = 48


def set_ends(entries, rng, low, largest):
    spot = [jax.random.randint(jax.random.fold_in(rng, axis), (), 0, length) for axis, length in enumerate(entries.shape)]
    widest = entries.shape.index(max(entries.shape))
    beside = spot[:widest] + [(spot[widest] + 1) % entries.shape[widest]] + spot[widest + 1:]
    return entries.at[tuple(spot)].set(low).at[tuple(beside)].set(largest)


def levels(own_key, shape, split, low, high):
    loudness, own = 1.0, jax.random.fold_in(own_key, 6)
    for axis_at, parts in split:
        draws = jnp.exp(jax.random.uniform(jax.random.fold_in(own, axis_at), (parts,), jnp.float32, low / len(split), high / len(split)))
        loudness = loudness * jnp.repeat(draws, shape[axis_at] // parts).reshape([-1 if axis == axis_at else 1 for axis in range(len(shape))])
    return loudness


def profile(amount, total, reach, slope):
    portions = [(1 << 20) // math.isqrt(rank ** slope) + 1 for rank in range(2, amount + 1)]
    spare, given = total - reach - (amount - 1), [1] * (amount - 1)
    while spare > 0:
        free = [i for i in range(amount - 1) if given[i] < reach]
        pool, remaining = sum([portions[i] for i in free]), spare
        for i in free:
            more = min(reach - given[i], max(1, remaining * portions[i] // pool), spare)
            given[i] = given[i] + more
            spare = spare - more
    return np.array([reach] + given)


def ragged(rng, number_of, total, bound, skew):
    if number_of == 2:
        one = jax.random.randint(rng, (), max(1, total - bound), min(bound, total - 1) + 1)
        return jnp.stack([one, total - one])
    lengths = jnp.asarray(profile(number_of, total, bound, skew), jnp.int32)
    pairs = (number_of - 1) // 2
    source_of, receiver = lengths[1:1 + 2 * pairs:2], lengths[2:2 + 2 * pairs:2]
    room = jnp.minimum(source_of - 1, bound - receiver)
    moved = jax.random.randint(jax.random.fold_in(rng, 1), (pairs,), 0, 1 << 20) % (room + 1)
    lengths = lengths.at[1:1 + 2 * pairs:2].set(source_of - moved).at[2:2 + 2 * pairs:2].set(receiver + moved)
    return lengths[jax.random.permutation(jax.random.fold_in(rng, 2), number_of)]


def bell_draw(key, dims, deviation, reach, cuts=(), held_as=jnp.bfloat16):
    values = deviation * jax.random.normal(key, dims, jnp.float32)
    if cuts:
        values = values * levels(key, dims, cuts, -0.22, 0.18)
    return jnp.clip(values, -reach, reach).astype(held_as)


def setup_inputs(seed: int = 0) -> dict:
    key_of = jax.random.split(jax.random.key(seed), 28)
    return {
        "tokens": bell_draw(key_of[0], (TOKENS, D), 1.0, 6.0, ((0, 32),)),
        "cotangent": bell_draw(key_of[1], (TOKENS, D), 1.0, 6.0, ((0, 32),)),
        "segments": jnp.searchsorted(jnp.cumsum(ragged(key_of[2], IMAGES, TOKENS, IMG_LEN, 1)), jnp.arange(TOKENS), side="right").astype(jnp.int32),
        "adapter_ids": set_ends(jax.random.randint(key_of[3], (IMAGES,), 0, ADAPTERS), jax.random.fold_in(key_of[3], 1), 0, ADAPTERS - 1).astype(jnp.int32),
        "ln1_gain": jnp.clip(1.0 + 0.1 * jax.random.normal(key_of[4], (D,), jnp.float32), 0.5, 1.5),
        "ln1_bias": bell_draw(key_of[5], (D,), 0.3, 1.5, (), jnp.float32),
        "w_query": bell_draw(key_of[6], (D, D), D ** -0.5, 0.1875, ((0, 32),)),
        "b_query": bell_draw(key_of[7], (D,), 0.5, 2.5, (), jnp.float32),
        "w_key": bell_draw(key_of[8], (D, D), D ** -0.5, 0.1875, ((0, 32),)),
        "w_value": bell_draw(key_of[9], (D, D), D ** -0.5, 0.1875, ((0, 32),)),
        "b_value": bell_draw(key_of[10], (D,), 0.5, 2.5, (), jnp.float32),
        "w_out": bell_draw(key_of[11], (D, D), (max(1, D // IMG_MEAN)) ** -0.5, 4.0, ((0, 32),)),
        "b_out": bell_draw(key_of[12], (D,), 0.5, 2.5, (), jnp.float32),
        "ln2_gain": jnp.clip(1.0 + 0.1 * jax.random.normal(key_of[13], (D,), jnp.float32), 0.5, 1.5),
        "ln2_bias": bell_draw(key_of[14], (D,), 0.3, 1.5, (), jnp.float32),
        "w_up": bell_draw(key_of[15], (D, FF), D ** -0.5, 0.1875, ((0, 32),)),
        "b_up": bell_draw(key_of[16], (FF,), 0.5, 2.5, (), jnp.float32),
        "w_down": bell_draw(key_of[17], (FF, D), (FF // 4) ** -0.5, 0.1875, ((0, 32),)),
        "b_down": bell_draw(key_of[18], (D,), 0.5, 2.5, (), jnp.float32),
        "query_in": bell_draw(key_of[19], (D, AR), D ** -0.5, 0.1875, ((0, 32),)),
        "query_out": bell_draw(key_of[20], (D, AR), (4 * RANK) ** -0.5, 0.75, ((0, 32),)),
        "value_in": bell_draw(key_of[21], (D, AR), D ** -0.5, 0.1875, ((0, 32),)),
        "value_out": bell_draw(key_of[22], (D, AR), (4 * RANK) ** -0.5, 0.75, ((0, 32),)),
        "up_in": bell_draw(key_of[23], (D, AR), D ** -0.5, 0.1875, ((0, 32),)),
        "up_out": bell_draw(key_of[24], (FF, AR), (4 * RANK) ** -0.5, 0.75, ((0, 32),)),
        "down_in": bell_draw(key_of[25], (FF, AR), (FF // 4) ** -0.5, 0.1875, ((0, 32),)),
        "down_out": bell_draw(key_of[26], (D, AR), (4 * RANK) ** -0.5, 0.75, ((0, 32),)),
    }


@jax.custom_vjp
def low(v):
    return lax.optimization_barrier(v.astype(jnp.bfloat16)).astype(jnp.float32)

@jax.custom_vjp
def low_back(v):
    return v

def low_keep(v):
    return (low(v), None)

def low_pass(kept, grad):
    return (grad,)

def back_keep(v):
    return (v, None)

def back_low(kept, grad):
    return (low(grad),)
low.defvjp(low_keep, low_pass)
low_back.defvjp(back_keep, back_low)
highest = lax.Precision.HIGHEST
epsilon = 1e-05
gelu_slope = 1.702

def matmul(left, right):
    return jnp.dot(left, right, precision=highest, preferred_element_type=jnp.float32)

def times_transposed(left, right):
    return lax.dot_general(left, right, (((1,), (1,)), ((), ())), precision=highest, preferred_element_type=jnp.float32)

def layer_norm(values, gain, shift):
    mean = lax.optimization_barrier(jnp.mean(values, axis=1, keepdims=True))
    centered = values - mean
    variance = lax.optimization_barrier(jnp.mean(centered * centered, axis=1, keepdims=True))
    return centered * lax.rsqrt(variance + epsilon) * gain + shift

def attend_block(query_rows, key_rows, value_rows, seg_query, seg_keys):
    row_count = query_rows.shape[0]
    key_count = key_rows.shape[0]
    head_dim = D // HEADS
    query3 = query_rows.reshape(row_count, HEADS, head_dim)
    key3 = key_rows.reshape(key_count, HEADS, head_dim)
    value3 = value_rows.reshape(key_count, HEADS, head_dim)
    scores = low_back(jnp.einsum('qhd,khd->hqk', query3, key3, precision=highest) * head_dim ** (-0.5))
    same_image = seg_query[:, None] == seg_keys[None, :]
    scores = jnp.where(same_image[None], scores, -1000000000.0)
    row_max = lax.optimization_barrier(jnp.max(scores, axis=2, keepdims=True))
    exp_scores = jnp.exp(scores - row_max)
    softmax_w = low(exp_scores / lax.optimization_barrier(jnp.sum(exp_scores, axis=2, keepdims=True)))
    attended = jnp.einsum('hqk,khd->qhd', softmax_w, value3, precision=highest)
    return attended.reshape(row_count, D)

def reference(tokens, cotangent, segments, adapter_ids, ln1_gain, ln1_bias, w_query, b_query, w_key, w_value, b_value, w_out, b_out, ln2_gain, ln2_bias, w_up, b_up, w_down, b_down, query_in, query_out, value_in, value_out, up_in, up_out, down_in, down_out):

    def to_float(array):
        return array.astype(jnp.float32)
    image_hot = (segments[:, None] == jnp.arange(IMAGES, dtype=jnp.int32)[None, :]).astype(jnp.float32)
    adapter_hot = (adapter_ids[:, None] == jnp.arange(ADAPTERS, dtype=jnp.int32)[None, :]).astype(jnp.float32)
    select = jnp.repeat(matmul(image_hot, adapter_hot), RANK, axis=1)
    padded_seg = jnp.pad(segments, HALO, constant_values=-1)
    block_count = TOKENS // TOK_DEV
    wq_f, wk_f, wv_f, wo_f = (to_float(w_query), to_float(w_key), to_float(w_value), to_float(w_out))
    wup_f, wdown_f = (to_float(w_up), to_float(w_down))

    def forward(inputs, q_in, q_out, v_in, v_out, u_in, u_out, d_in, d_out):
        normed1 = low(layer_norm(inputs, ln1_gain, ln1_bias))
        low_q = low_back(low(select * matmul(normed1, q_in)))
        low_v = low_back(low(select * matmul(normed1, v_in)))
        query = low_back(low(matmul(normed1, wq_f) + b_query + times_transposed(low_q, q_out)))
        keys = low_back(low(matmul(normed1, wk_f)))
        values = low_back(low(matmul(normed1, wv_f) + b_value + times_transposed(low_v, v_out)))
        padded_keys = jnp.pad(keys, ((HALO, HALO), (0, 0)))
        padded_values = jnp.pad(values, ((HALO, HALO), (0, 0)))

        def one_block(index):
            start = index * TOK_DEV
            query_rows = lax.dynamic_slice_in_dim(query, start, TOK_DEV, 0)
            key_rows = lax.dynamic_slice_in_dim(padded_keys, start, TOK_DEV + 2 * HALO, 0)
            value_rows = lax.dynamic_slice_in_dim(padded_values, start, TOK_DEV + 2 * HALO, 0)
            seg_query = lax.dynamic_slice_in_dim(segments, start, TOK_DEV, 0)
            seg_keys = lax.dynamic_slice_in_dim(padded_seg, start, TOK_DEV + 2 * HALO, 0)
            return attend_block(query_rows, key_rows, value_rows, seg_query, seg_keys)
        attended = lax.map(jax.checkpoint(one_block), jnp.arange(block_count, dtype=jnp.int32))
        mixed = low_back(low(attended.reshape(TOKENS, D)))
        branch = low_back(matmul(mixed, wo_f) + b_out)
        resid = inputs + branch
        normed2 = low(layer_norm(resid, ln2_gain, ln2_bias))
        low_u = low_back(low(select * matmul(normed2, u_in)))
        pre = low_back(matmul(normed2, wup_f) + b_up + times_transposed(low_u, u_out))
        gate = 1.0 / (1.0 + jnp.exp(-gelu_slope * pre))
        act = low(pre * gate)
        low_d = low_back(low(select * matmul(act, d_in)))
        return resid + matmul(act, wdown_f) + b_down + times_transposed(low_d, d_out)
    result, pullback = jax.vjp(forward, to_float(tokens), to_float(query_in), to_float(query_out), to_float(value_in), to_float(value_out), to_float(up_in), to_float(up_out), to_float(down_in), to_float(down_out))
    grads = pullback(to_float(cotangent))
    return (result.astype(jnp.bfloat16), grads[0].astype(jnp.bfloat16), grads[1], grads[2], grads[3], grads[4], grads[5], grads[6], grads[7], grads[8])
```

```python
import functools

import jax
import jax.numpy as jnp
from jax import lax
from jax.experimental import pallas as pl
from jax.experimental.pallas import tpu as pltpu
from jax.sharding import PartitionSpec as P

HEADS = 16
IMG_LEN = 577
RANK = 16
ADAPTERS = 8
EPS = 1e-05
SLOPE = 1.702
NEG = -1000000000.0
AXES = ("fsdp", "dp")
LANES = 128
TILE = 256
HALO = 640
VMEM_LIMIT = 60 * 1024 * 1024

f32 = jnp.float32
bf16 = jnp.bfloat16


def dot_nn(a, b):
    return jnp.dot(a, b, preferred_element_type=f32)


def dot_nt(a, b):
    return lax.dot_general(a, b, (((1,), (1,)), ((), ())), preferred_element_type=f32)


def dot_tn(a, b):
    return lax.dot_general(a, b, (((0,), (0,)), ((), ())), preferred_element_type=f32)


def norm_forward(values, gain, shift):
    mean = jnp.mean(values, axis=1, keepdims=True)
    centered = values - mean
    inverse = lax.rsqrt(jnp.mean(centered * centered, axis=1, keepdims=True) + EPS)
    normed = centered * inverse
    return normed * gain + shift, normed, inverse


def norm_backward(grad, normed, inverse, gain):
    scaled = grad * gain
    return inverse * (
        scaled
        - jnp.mean(scaled, axis=1, keepdims=True)
        - normed * jnp.mean(scaled * normed, axis=1, keepdims=True)
    )


def params(grid_dims):
    return pltpu.CompilerParams(
        dimension_semantics=("arbitrary",) * grid_dims, vmem_limit_bytes=VMEM_LIMIT
    )


def whole(shape):
    return pl.BlockSpec(shape, lambda *_: (0,) * len(shape), pipeline_mode=pl.Buffered(1))


def twice(x):
    return jnp.concatenate([x, x], axis=1)


def qkv_kernel(tok, sel, w, bq, bv, gain, shift, q_o, k_o, v_o):
    width = tok.shape[1]
    normal, _, _ = norm_forward(tok[...].astype(f32), gain[...], shift[...])
    n1 = normal.astype(bf16)
    select = sel[...]
    low = dot_nn(n1, w[:, 3 * width : 3 * width + 2 * LANES]).astype(bf16)
    low_q = low[:, :LANES] * select
    low_v = low[:, LANES:] * select
    q_out = w[:, 3 * width + 2 * LANES : 3 * width + 3 * LANES]
    v_out = w[:, 3 * width + 3 * LANES : 3 * width + 4 * LANES]
    scale = (width // HEADS) ** -0.5
    q = dot_nn(n1, w[:, :width]) + bq[...] + dot_nt(low_q, q_out)
    q_o[...] = (q * scale).astype(bf16)
    k_o[...] = dot_nn(n1, w[:, width : 2 * width]).astype(bf16)
    v = dot_nn(n1, w[:, 2 * width : 3 * width]) + bv[...] + dot_nt(low_v, v_out)
    v_o[...] = v.astype(bf16)


def qkv_call(tok_w, sel_w, w_a, bq, bv, gain, shift):
    rows, width = tok_w.shape
    tile = pl.BlockSpec((TILE, width), lambda i: (i, 0))
    vec = whole((1, width))
    out = jax.ShapeDtypeStruct((rows, width), bf16)
    return pl.pallas_call(
        qkv_kernel,
        grid=(rows // TILE,),
        in_specs=[
            tile,
            pl.BlockSpec((TILE, LANES), lambda i: (i, 0)),
            whole(w_a.shape),
            vec,
            vec,
            vec,
            vec,
        ],
        out_specs=[tile] * 3,
        out_shape=[out] * 3,
        compiler_params=params(1),
        name="qkv",
    )(tok_w, sel_w, w_a, bq, bv, gain, shift)


def head_masks(rows):
    lane = lax.broadcasted_iota(jnp.int32, (rows, LANES), 1)
    return lane < (LANES // 2)


def attend_kernel(tab, q, k, v, segc, segr, mixed_o, lse_o, s_scr):
    own = mixed_o.shape[0]
    first = head_masks(TILE)
    zero = jnp.zeros((), bf16)
    one = jnp.ones((), bf16)
    for i in range(own // TILE):
        start, count = tab[2 * i], tab[2 * i + 1]
        row = HALO + TILE * i
        qt = q[row : row + TILE, :]
        q0 = jnp.where(first, qt, zero)
        q1 = jnp.where(first, zero, qt)
        sq = twice(segc[row : row + TILE, :])

        def scores(t, carry):
            m0, m1 = carry
            at = start + 2 * t
            kt = k[pl.ds(pl.multiple_of(at * LANES, LANES), TILE), :]
            sk = jnp.concatenate([segr[pl.ds(at, 1), :], segr[pl.ds(at + 1, 1), :]], axis=1)
            mask = sq == sk
            s0 = jnp.where(mask, dot_nt(q0, kt), NEG)
            s1 = jnp.where(mask, dot_nt(q1, kt), NEG)
            s_scr[0, t] = s0
            s_scr[1, t] = s1
            m0 = jnp.maximum(m0, jnp.maximum(s0[:, :LANES], s0[:, LANES:]))
            m1 = jnp.maximum(m1, jnp.maximum(s1[:, :LANES], s1[:, LANES:]))
            return m0, m1

        low = jnp.full((TILE, LANES), NEG, f32)
        m0, m1 = lax.fori_loop(0, count, scores, (low, low))
        m0 = jnp.max(m0, axis=1, keepdims=True)
        m1 = jnp.max(m1, axis=1, keepdims=True)

        def weigh(t, carry):
            a0, a1 = carry
            at = start + 2 * t
            vt = v[pl.ds(pl.multiple_of(at * LANES, LANES), TILE), :]
            p0 = jnp.exp(s_scr[0, t] - m0).astype(bf16)
            p1 = jnp.exp(s_scr[1, t] - m1).astype(bf16)
            a0 = a0 + dot_nn(p0, jnp.where(first, vt, one))
            a1 = a1 + dot_nn(p1, jnp.where(first, one, vt))
            return a0, a1

        empty = jnp.zeros((TILE, LANES), f32)
        a0, a1 = lax.fori_loop(0, count, weigh, (empty, empty))
        r0 = pltpu.roll(a0, LANES // 2, 1)
        r1 = pltpu.roll(a1, LANES // 2, 1)
        mixed_o[TILE * i : TILE * (i + 1), :] = jnp.where(first, a0 / r0, a1 / r1).astype(bf16)
        l0 = (m0 + jnp.log(jnp.where(first, r0, a0))).T
        l1 = (m1 + jnp.log(jnp.where(first, a1, r1))).T
        for half in range(2):
            at = 2 * i + half
            lse_o[0, 0, at : at + 1, :] = l0[0:1, half * LANES : (half + 1) * LANES]
            lse_o[0, 1, at : at + 1, :] = l1[0:1, half * LANES : (half + 1) * LANES]


def attend_call(tab, q, k, v, segc, segr, own):
    rows, width = q.shape
    pairs = width // LANES
    col = pl.BlockSpec((rows, LANES), lambda h, *_: (0, h))
    return pl.pallas_call(
        attend_kernel,
        grid_spec=pltpu.PrefetchScalarGridSpec(
            num_scalar_prefetch=1,
            grid=(pairs,),
            in_specs=[col, col, col, whole(segc.shape), whole(segr.shape)],
            out_specs=[
                pl.BlockSpec((own, LANES), lambda h, *_: (0, h)),
                pl.BlockSpec((1, 2, own // LANES, LANES), lambda h, *_: (h, 0, 0, 0)),
            ],
            scratch_shapes=[pltpu.VMEM((2, rows // TILE, TILE, TILE), f32)],
        ),
        out_shape=[
            jax.ShapeDtypeStruct((own, width), bf16),
            jax.ShapeDtypeStruct((pairs, 2, own // LANES, LANES), f32),
        ],
        compiler_params=params(1),
        name="attend",
    )(tab, q, k, v, segc, segr)


def split_pair(x, first):
    zero = jnp.zeros((), bf16)
    return jnp.concatenate([jnp.where(first, x, zero), jnp.where(first, zero, x)], axis=0)


def pair_grads(kt, vt, qcat, dcat, mask, lse0, lse1, dlt0, dlt1):
    half = qcat.shape[0] // 2
    s = dot_nt(kt, qcat)
    dp = dot_nt(vt, dcat)
    p0 = jnp.exp(jnp.where(mask, s[:, :half], NEG) - lse0)
    p1 = jnp.exp(jnp.where(mask, s[:, half:], NEG) - lse1)
    d0 = (p0 * (dp[:, :half] - dlt0)).astype(bf16)
    d1 = (p1 * (dp[:, half:] - dlt1)).astype(bf16)
    probs = jnp.concatenate([p0.astype(bf16), p1.astype(bf16)], axis=1)
    return probs, d0, d1


def attend_back_kernel(tab, q, k, v, dm, lse, dlt, segc, segr, dq_o, dk_o, dv_o, dk_a, dv_a):
    own = dm.shape[0]
    first = head_masks(TILE)
    scale = (LANES // 2) ** -0.5
    dk_a[...] = jnp.zeros_like(dk_a)
    dv_a[...] = jnp.zeros_like(dv_a)
    for i in range(own // TILE):
        start, count = tab[2 * i], tab[2 * i + 1]
        row = HALO + TILE * i
        qcat = split_pair(q[row : row + TILE, :], first)
        dcat = split_pair(dm[TILE * i : TILE * (i + 1), :], first)

        def line(ref, head):
            return jnp.concatenate(
                [ref[0, head, 2 * i : 2 * i + 1, :], ref[0, head, 2 * i + 1 : 2 * i + 2, :]], axis=1
            )

        lse0, lse1, dlt0, dlt1 = line(lse, 0), line(lse, 1), line(dlt, 0), line(dlt, 1)
        at_q = row // LANES
        sq = jnp.concatenate([segr[at_q : at_q + 1, :], segr[at_q + 1 : at_q + 2, :]], axis=1)

        def step(t, carry):
            a0, a1 = carry
            at = pl.multiple_of((start + 2 * t) * LANES, LANES)
            kt = k[pl.ds(at, TILE), :]
            vt = v[pl.ds(at, TILE), :]
            mask = twice(segc[pl.ds(at, TILE), :]) == sq
            probs, d0, d1 = pair_grads(kt, vt, qcat, dcat, mask, lse0, lse1, dlt0, dlt1)
            dv_a[pl.ds(at, TILE), :] += dot_nn(probs, dcat)
            dk_a[pl.ds(at, TILE), :] += dot_nn(jnp.concatenate([d0, d1], axis=1), qcat)
            return a0 + dot_tn(d0, kt), a1 + dot_tn(d1, kt)

        empty = jnp.zeros((TILE, LANES), f32)
        a0, a1 = lax.fori_loop(0, count, step, (empty, empty))
        dq_o[TILE * i : TILE * (i + 1), :] = (jnp.where(first, a0, a1) * scale).astype(bf16)
    dk_o[...] = dk_a[HALO : HALO + own, :]
    dv_o[...] = dv_a[HALO : HALO + own, :]


def attend_back_call(tab, q, k, v, dm, lse, dlt, segc, segr):
    rows, width = q.shape
    own = dm.shape[0]
    pairs = width // LANES
    col = pl.BlockSpec((rows, LANES), lambda h, *_: (0, h))
    own_col = pl.BlockSpec((own, LANES), lambda h, *_: (0, h))
    stat = pl.BlockSpec((1, 2, own // LANES, LANES), lambda h, *_: (h, 0, 0, 0))
    return pl.pallas_call(
        attend_back_kernel,
        grid_spec=pltpu.PrefetchScalarGridSpec(
            num_scalar_prefetch=1,
            grid=(pairs,),
            in_specs=[col, col, col, own_col, stat, stat, whole(segc.shape), whole(segr.shape)],
            out_specs=[own_col] * 3,
            scratch_shapes=[pltpu.VMEM((rows, LANES), f32)] * 2,
        ),
        out_shape=[
            jax.ShapeDtypeStruct((own, width), bf16),
            jax.ShapeDtypeStruct((own, width), f32),
            jax.ShapeDtypeStruct((own, width), f32),
        ],
        compiler_params=params(1),
        name="attend_back",
    )(tab, q, k, v, dm, lse, dlt, segc, segr)


def halo_back_kernel(
    tab, q, k, v, dm_l, dm_r, st_l, st_r, dk_i, dv_i, segc, segr, dk_o, dv_o, dk_a, dv_a
):
    own = dk_o.shape[0]
    first = head_masks(LANES)
    dk_a[...] = dk_i[...]
    dv_a[...] = dv_i[...]
    for side in range(2):
        base = 6 + 3 * side
        count_q, k_first, count_k = tab[base], tab[base + 1], tab[base + 2]
        dm, st = (dm_l, st_l) if side == 0 else (dm_r, st_r)

        def query_tile(t, carry):
            tile = HALO // LANES - 1 - t if side == 0 else t
            tile_w = tile if side == 0 else tile + (HALO + own) // LANES
            at_h = pl.multiple_of(tile * LANES, LANES)
            at_w = pl.multiple_of(tile_w * LANES, LANES)
            qcat = split_pair(q[pl.ds(at_w, LANES), :], first)
            dcat = split_pair(dm[pl.ds(at_h, LANES), :], first)
            lse0, lse1 = st[0, 0, 0, pl.ds(tile, 1), :], st[0, 0, 1, pl.ds(tile, 1), :]
            dlt0, dlt1 = st[1, 0, 0, pl.ds(tile, 1), :], st[1, 0, 1, pl.ds(tile, 1), :]
            sq = segr[pl.ds(tile_w, 1), :]

            def key_tile(u, inner):
                at = pl.multiple_of((k_first + u) * TILE, TILE)
                at_k = pl.multiple_of(HALO + at, LANES)
                kt = k[pl.ds(at_k, TILE), :]
                vt = v[pl.ds(at_k, TILE), :]
                mask = segc[pl.ds(at_k, TILE), :] == sq
                probs, d0, d1 = pair_grads(kt, vt, qcat, dcat, mask, lse0, lse1, dlt0, dlt1)
                dv_a[pl.ds(at, TILE), :] += dot_nn(probs, dcat)
                dk_a[pl.ds(at, TILE), :] += dot_nn(jnp.concatenate([d0, d1], axis=1), qcat)
                return inner

            return lax.fori_loop(0, count_k, key_tile, carry)

        lax.fori_loop(0, count_q, query_tile, 0)
    dk_o[...] = dk_a[...].astype(bf16)
    dv_o[...] = dv_a[...].astype(bf16)


def halo_back_call(tab, q, k, v, dm_l, dm_r, st_l, st_r, dk, dv, segc, segr):
    rows, width = q.shape
    own = dk.shape[0]
    pairs = width // LANES
    col = pl.BlockSpec((rows, LANES), lambda h, *_: (0, h))
    own_col = pl.BlockSpec((own, LANES), lambda h, *_: (0, h))
    halo_col = pl.BlockSpec((HALO, LANES), lambda h, *_: (0, h))
    stat = pl.BlockSpec((2, 1, 2, HALO // LANES, LANES), lambda h, *_: (0, h, 0, 0, 0))
    return pl.pallas_call(
        halo_back_kernel,
        grid_spec=pltpu.PrefetchScalarGridSpec(
            num_scalar_prefetch=1,
            grid=(pairs,),
            in_specs=[
                col,
                col,
                col,
                halo_col,
                halo_col,
                stat,
                stat,
                own_col,
                own_col,
                whole(segc.shape),
                whole(segr.shape),
            ],
            out_specs=[own_col] * 2,
            scratch_shapes=[pltpu.VMEM((own, LANES), f32)] * 2,
        ),
        out_shape=[jax.ShapeDtypeStruct((own, width), bf16)] * 2,
        compiler_params=params(1),
        name="halo_back",
    )(tab, q, k, v, dm_l, dm_r, st_l, st_r, dk, dv, segc, segr)


FF_TILE = 512


def mlp_kernel(
    mixed, tok, dy, sel, w_out, w_up, w_lo, w_dn, b_out, b_up, b_down, gain, shift, heads,
    out_o, dres_o, dmix_o, dlt_o, gui_o, gdo_o, guo_o, gdi_o,
    resid, n2, low_u, dlow_d, low_ut, dlow_dt, acc, acc_low, dn2, dlow_u, gdo_t, gui_t,
):
    j = pl.program_id(0)
    rows, width = mixed.shape
    chunks = [pl.ds(r, TILE) for r in range(0, rows, TILE)]
    up_in = w_lo[:, :LANES]
    down_out = w_lo[:, LANES:]

    @pl.when(j == 0)
    def _():
        for r in chunks:
            x = tok[r, :].astype(f32) + dot_nn(mixed[r, :], w_out[...]) + b_out[...]
            resid[r, :] = x
            normal, _, _ = norm_forward(x, gain[...], shift[...])
            normal = normal.astype(bf16)
            n2[r, :] = normal
            lu = dot_nn(normal, up_in).astype(bf16) * sel[r, :]
            ld = dot_nn(dy[r, :], down_out).astype(bf16) * sel[r, :]
            low_u[r, :] = lu
            dlow_d[r, :] = ld
            low_ut[:, r] = lu.astype(f32).T.astype(bf16)
            dlow_dt[:, r] = ld.astype(f32).T.astype(bf16)
        acc[...] = jnp.zeros_like(acc)
        acc_low[...] = jnp.zeros_like(acc_low)
        dn2[...] = jnp.zeros_like(dn2)
        dlow_u[...] = jnp.zeros_like(dlow_u)
        gdo_t[...] = jnp.zeros_like(gdo_t)
        gui_t[...] = jnp.zeros_like(gui_t)

    down = w_dn[:, :width]
    up_out = w_dn[:, width : width + LANES]
    down_in = w_dn[:, width + LANES :]
    guo_t = jnp.zeros((LANES, FF_TILE), f32)
    gdi_t = jnp.zeros((LANES, FF_TILE), f32)
    for r in chunks:
        pre = dot_nn(n2[r, :], w_up[...]) + b_up[...] + dot_nt(low_u[r, :], up_out)
        d_act = dot_nt(dy[r, :], down) + dot_nt(dlow_d[r, :], down_in)
        gate = 1.0 / (1.0 + jnp.exp(-SLOPE * pre))
        act = pre * gate
        d_pre = (d_act * (gate + SLOPE * act * (1.0 - gate))).astype(bf16)
        act = act.astype(bf16)
        acc[r, :] += dot_nn(act, down)
        acc_low[r, :] += dot_nn(act, down_in)
        dn2[r, :] += dot_nt(d_pre, w_up[...])
        dlow_u[r, :] += dot_nn(d_pre, up_out)
        guo_t += dot_nn(low_ut[:, r], d_pre)
        gdi_t += dot_nn(dlow_dt[:, r], act)
    guo_o[...] = guo_t.T
    gdi_o[...] = gdi_t.T

    @pl.when(j == pl.num_programs(0) - 1)
    def _():
        for r in chunks:
            select = sel[r, :]
            x = resid[r, :]
            low_d = acc_low[r, :].astype(bf16) * select
            out_o[r, :] = (x + acc[r, :] + b_down[...] + dot_nt(low_d, down_out)).astype(bf16)
            lu = dlow_u[r, :].astype(bf16) * select
            _, hat, inv = norm_forward(x, gain[...], shift[...])
            grad = dn2[r, :] + dot_nt(lu, up_in)
            dres = dy[r, :].astype(f32) + norm_backward(grad, hat, inv, gain[...])
            dres_o[r, :] = dres
            dmix = dot_nt(dres.astype(bf16), w_out[...]).astype(bf16)
            dmix_o[r, :] = dmix
            prod = dmix.astype(f32) * mixed[r, :].astype(f32)
            high = prod.astype(bf16)
            rest = (prod - high.astype(f32)).astype(bf16)
            dlt_o[:, r] = dot_nt(heads[...], high) + dot_nt(heads[...], rest)
            gdo_t[...] += dot_nn(low_d.astype(f32).T.astype(bf16), dy[r, :])
            gui_t[...] += dot_nn(lu.astype(f32).T.astype(bf16), n2[r, :])
        gdo_o[...] = gdo_t[...].T
        gui_o[...] = gui_t[...].T


def mlp_call(mixed, tok, dy, sel, w_b, w_c, b_out, b_up, b_down, gain, shift, heads):
    rows, width = mixed.shape
    hidden = w_c.shape[0]
    full = whole((rows, width))
    vec = whole((1, width))
    low = whole((rows, LANES))
    lead = width // FF_TILE
    at_low = (width + hidden) // (2 * LANES)
    grads = jax.ShapeDtypeStruct((width, LANES), f32)
    grads_ff = jax.ShapeDtypeStruct((hidden, LANES), f32)
    const = lambda shape: pl.BlockSpec(shape, lambda j: (0,) * len(shape))
    ff_rows = pl.BlockSpec((FF_TILE, LANES), lambda j: (j, 0))
    return pl.pallas_call(
        mlp_kernel,
        grid=(hidden // FF_TILE,),
        in_specs=[
            full,
            full,
            full,
            low,
            whole((width, width)),
            pl.BlockSpec((width, FF_TILE), lambda j: (0, lead + j)),
            pl.BlockSpec((width, 2 * LANES), lambda j: (0, at_low), pipeline_mode=pl.Buffered(1)),
            pl.BlockSpec((FF_TILE, w_c.shape[1]), lambda j: (j, 0)),
            vec,
            pl.BlockSpec((1, FF_TILE), lambda j: (0, j)),
            vec,
            vec,
            vec,
            whole(heads.shape),
        ],
        out_specs=[
            const((rows, width)),
            const((rows, width)),
            const((rows, width)),
            const((HEADS, rows)),
            const((width, LANES)),
            const((width, LANES)),
            ff_rows,
            ff_rows,
        ],
        out_shape=[
            jax.ShapeDtypeStruct((rows, width), bf16),
            jax.ShapeDtypeStruct((rows, width), f32),
            jax.ShapeDtypeStruct((rows, width), bf16),
            jax.ShapeDtypeStruct((HEADS, rows), f32),
            grads,
            grads,
            grads_ff,
            grads_ff,
        ],
        scratch_shapes=[
            pltpu.VMEM((rows, width), f32),
            pltpu.VMEM((rows, width), bf16),
            pltpu.VMEM((rows, LANES), bf16),
            pltpu.VMEM((rows, LANES), bf16),
            pltpu.VMEM((LANES, rows), bf16),
            pltpu.VMEM((LANES, rows), bf16),
            pltpu.VMEM((rows, width), f32),
            pltpu.VMEM((rows, LANES), f32),
            pltpu.VMEM((rows, width), f32),
            pltpu.VMEM((rows, LANES), f32),
            pltpu.VMEM((LANES, width), f32),
            pltpu.VMEM((LANES, width), f32),
        ],
        compiler_params=params(1),
        name="mlp",
    )(mixed, tok, dy, sel, w_b, w_b, w_b, w_c, b_out, b_up, b_down, gain, shift, heads)


def qkv_back_kernel(dq, dk, dv, tok, dres, sel, w, gain, shift, gin_o, grads_o, acc):
    i = pl.program_id(0)
    width = tok.shape[1]
    normal, hat, inv = norm_forward(tok[...].astype(f32), gain[...], shift[...])
    n1 = normal.astype(bf16)
    select = sel[...]
    q_in = w[:, 3 * width : 3 * width + LANES]
    v_in = w[:, 3 * width + LANES : 3 * width + 2 * LANES]
    q_out = w[:, 3 * width + 2 * LANES : 3 * width + 3 * LANES]
    v_out = w[:, 3 * width + 3 * LANES : 3 * width + 4 * LANES]
    low_q = dot_nn(n1, q_in).astype(bf16) * select
    low_v = dot_nn(n1, v_in).astype(bf16) * select
    dlow_q = dot_nn(dq[...], q_out).astype(bf16) * select
    dlow_v = dot_nn(dv[...], v_out).astype(bf16) * select
    grad = (
        dot_nt(dq[...], w[:, :width])
        + dot_nt(dk[...], w[:, width : 2 * width])
        + dot_nt(dv[...], w[:, 2 * width : 3 * width])
        + dot_nt(dlow_q, q_in)
        + dot_nt(dlow_v, v_in)
    )
    gin_o[...] = (dres[...] + norm_backward(grad, hat, inv, gain[...])).astype(bf16)

    @pl.when(i == 0)
    def _():
        acc[...] = jnp.zeros_like(acc)

    def turned(x):
        return x.astype(f32).T.astype(bf16)

    acc[0] += dot_nn(turned(dlow_q), n1)
    acc[1] += dot_nn(turned(low_q), dq[...])
    acc[2] += dot_nn(turned(dlow_v), n1)
    acc[3] += dot_nn(turned(low_v), dv[...])

    @pl.when(i == pl.num_programs(0) - 1)
    def _():
        for at in range(4):
            grads_o[at] = acc[at].T


def qkv_back_call(dq, dk, dv, tok, dres, sel, w_a, gain, shift):
    rows, width = tok.shape
    tile = pl.BlockSpec((TILE, width), lambda i: (i, 0))
    vec = whole((1, width))
    return pl.pallas_call(
        qkv_back_kernel,
        grid=(rows // TILE,),
        in_specs=[
            tile,
            tile,
            tile,
            tile,
            tile,
            pl.BlockSpec((TILE, LANES), lambda i: (i, 0)),
            whole(w_a.shape),
            vec,
            vec,
        ],
        out_specs=[tile, pl.BlockSpec((4, width, LANES), lambda i: (0, 0, 0))],
        out_shape=[
            jax.ShapeDtypeStruct((rows, width), bf16),
            jax.ShapeDtypeStruct((4, width, LANES), f32),
        ],
        scratch_shapes=[pltpu.VMEM((4, LANES, width), f32)],
        compiler_params=params(1),
        name="qkv_back",
    )(dq, dk, dv, tok, dres, sel, w_a, gain, shift)


def halved(parts, devices, inner):
    me = lax.axis_index(AXES)
    bits = devices.bit_length() - 1
    core = inner.bit_length() - 1
    order = [core] + list(range(core)) + [b for b in range(bits) if b > core]
    left = list(range(bits))[::-1]
    parts = [p.reshape(devices, -1, p.shape[-1]) for p in parts]
    x = parts
    for step, bit in enumerate(order):
        at = left.index(bit)
        outer, rest = 2**at, 2 ** (len(left) - 1 - at)
        mine = (me >> bit) & 1
        pairs = [(p, p ^ (1 << bit)) for p in range(devices)]

        def half(index):
            pieces = [
                lax.dynamic_index_in_dim(
                    p.reshape(outer, 2, rest, p.shape[1], p.shape[2]), index, 1, keepdims=False
                ).reshape(outer * rest, p.shape[1], p.shape[2])
                for p in x
            ]
            return pieces[0] if len(pieces) == 1 else jnp.concatenate(pieces, axis=1)

        send = half(1 - mine)
        if step > 0:
            send = send.astype(bf16)
        got = lax.ppermute(send, AXES, pairs)
        x = [half(mine) + got.astype(f32)]
        left.remove(bit)
    return x[0][0]


def local(
    tokens, cotangent, segments, adapter_ids, ln1_gain, ln1_bias, w_query, b_query, w_key, w_value,
    b_value, w_out, b_out, ln2_gain, ln2_bias, w_up, b_up, w_down, b_down, query_in, query_out,
    value_in, value_out, up_in, up_out, down_in, down_out,
):
    own, width = tokens.shape
    inner = lax.axis_size("dp")
    devices = lax.axis_size("fsdp") * inner
    up = [(i, i + 1) for i in range(devices - 1)]
    down = [(i + 1, i) for i in range(devices - 1)]

    def gather(*pieces):
        return lax.all_gather(jnp.concatenate(pieces, axis=1), AXES, axis=0, tiled=True)

    before = lax.ppermute(tokens[own - HALO :], AXES, up)
    after = lax.ppermute(tokens[:HALO], AXES, down)
    w_a = gather(w_query, w_key, w_value, query_in, value_in, query_out, value_out)
    w_b = gather(w_out, w_up, up_in, down_out)
    w_c = gather(w_down, up_out, down_in)

    position = lax.axis_index(AXES)
    padded = jnp.concatenate(
        [
            jnp.full((HALO,), -1, jnp.int32),
            segments,
            jnp.full((HALO,), 1 << 30, jnp.int32),
        ]
    )
    rows = own + 2 * HALO
    seg_w = lax.dynamic_slice_in_dim(padded, position * own, rows, 0)
    tile_seg = seg_w[HALO : HALO + own].reshape(own // TILE, TILE)
    images = jnp.concatenate([tile_seg[:, 0], tile_seg[:, -1]])
    low = jnp.sum((seg_w[None, :] < images[:, None]).astype(jnp.int32), axis=1)
    high = jnp.sum((seg_w[None, :] <= images[:, None]).astype(jnp.int32), axis=1)
    tiles = own // TILE
    entries = []
    for i in range(tiles):
        start = low[i] // LANES
        count = (high[tiles + i] - start * LANES + TILE - 1) // TILE
        entries += [jnp.minimum(start, rows // LANES - 2 * count), count]
    count_l = (HALO - low[0] + LANES - 1) // LANES
    entries += [
        jnp.maximum(count_l, 0),
        jnp.zeros((), jnp.int32),
        (jnp.minimum(high[0], HALO + own) - HALO + TILE - 1) // TILE,
    ]
    last = 2 * tiles - 1
    first_k = jnp.maximum(low[last] - HALO, 0) // TILE
    entries += [
        jnp.maximum((high[last] - HALO - own + LANES - 1) // LANES, 0),
        first_k,
        tiles - first_k,
    ]
    tab = jnp.stack(entries)
    segr = seg_w.reshape(rows // LANES, LANES)
    segc = jnp.broadcast_to(seg_w[:, None], (rows, LANES))

    image_hot = (seg_w[:, None] == jnp.arange(adapter_ids.shape[0], dtype=jnp.int32)).astype(bf16)
    column = jnp.arange(ADAPTERS * RANK, dtype=jnp.int32) // RANK
    adapter_hot = (adapter_ids[:, None] == column[None, :]).astype(bf16)
    sel_w = dot_nn(image_hot, adapter_hot).astype(bf16)
    sel = sel_w[HALO : HALO + own]
    heads = (
        jnp.arange(width, dtype=jnp.int32)[None, :] // (width // HEADS)
        == jnp.arange(HEADS, dtype=jnp.int32)[:, None]
    ).astype(bf16)

    row = lambda x: x.reshape(1, -1)
    tok_w = jnp.concatenate([before, tokens, after], axis=0)
    q, k, v = qkv_call(
        tok_w, sel_w, w_a, row(b_query), row(b_value), row(ln1_gain), row(ln1_bias)
    )
    mixed, lse = attend_call(tab, q, k, v, segc, segr, own)
    block_out, d_resid, d_mixed, delta, g_ui, g_do, g_uo, g_di = mlp_call(
        mixed, tokens, cotangent, sel, w_b, w_c, row(b_out), row(b_up), row(b_down),
        row(ln2_gain), row(ln2_bias), heads,
    )
    dlt = delta.reshape(lse.shape)
    stats = jnp.stack([lse, dlt])
    cut = (own - HALO) // LANES
    dm_l = lax.ppermute(d_mixed[own - HALO :], AXES, up)
    dm_r = lax.ppermute(d_mixed[:HALO], AXES, down)
    st_l = lax.ppermute(stats[:, :, :, cut:], AXES, up)
    st_r = lax.ppermute(stats[:, :, :, : HALO // LANES], AXES, down)
    mlp_grads = halved([g_ui, g_uo, g_di, g_do], devices, inner)
    dq, dk, dv = attend_back_call(tab, q, k, v, d_mixed, lse, dlt, segc, segr)
    dk, dv = halo_back_call(tab, q, k, v, dm_l, dm_r, st_l, st_r, dk, dv, segc, segr)
    grad_input, g_qv = qkv_back_call(
        dq, dk, dv, tokens, d_resid, sel, w_a, row(ln1_gain), row(ln1_bias)
    )
    qv_grads = halved([g_qv[0], g_qv[1], g_qv[2], g_qv[3]], devices, inner)
    r = width // devices
    r_ff = w_c.shape[0] // devices
    return (
        block_out,
        grad_input,
        qv_grads[:r],
        qv_grads[r : 2 * r],
        qv_grads[2 * r : 3 * r],
        qv_grads[3 * r :],
        mlp_grads[:r],
        mlp_grads[r : r + r_ff],
        mlp_grads[r + r_ff : r + 2 * r_ff],
        mlp_grads[r + 2 * r_ff :],
    )


def solution(mesh):
    split = P(AXES, None)
    return jax.shard_map(
        local,
        mesh=mesh,
        in_specs=(
            split, split, P(), P(), P(), P(), split, P(), split, split, P(), split, P(), P(), P(),
            split, P(), split, P(), split, split, split, split, split, split, split, split,
        ),
        out_specs=(split,) * 10,
        check_vma=False,
    )
```

```python
import jax
import jax.numpy as jnp
from jax import lax
from jax.experimental import pallas as pl
from jax.experimental.pallas import tpu as pltpu
from jax.sharding import PartitionSpec as P


HEADS = 16
RANK = 16
ADAPTERS = 8
EPS = 1e-05
SLOPE = 1.702
NEG = -1000000000.0
AXES = ("fsdp", "dp")
LANES = 128
TILE = 256
HALO = 640
VMEM_LIMIT = 60 * 1024 * 1024
WIDE = 2

f32 = jnp.float32
bf16 = jnp.bfloat16


def dot_nn(a, b):
    return jnp.dot(a, b, preferred_element_type=f32)


def dot_nt(a, b):
    return lax.dot_general(a, b, (((1,), (1,)), ((), ())), preferred_element_type=f32)


def dot_tn(a, b):
    return lax.dot_general(a, b, (((0,), (0,)), ((), ())), preferred_element_type=f32)


def norm_forward(values, gain, shift):
    mean = jnp.mean(values, axis=1, keepdims=True)
    centered = values - mean
    inverse = lax.rsqrt(jnp.mean(centered * centered, axis=1, keepdims=True) + EPS)
    normed = centered * inverse
    return normed * gain + shift, normed, inverse


def norm_backward(grad, normed, inverse, gain):
    scaled = grad * gain
    return inverse * (
        scaled
        - jnp.mean(scaled, axis=1, keepdims=True)
        - normed * jnp.mean(scaled * normed, axis=1, keepdims=True)
    )


def params(grid_dims):
    return pltpu.CompilerParams(
        dimension_semantics=("arbitrary",) * grid_dims, vmem_limit_bytes=VMEM_LIMIT
    )


def whole(shape):
    return pl.BlockSpec(shape, lambda *_: (0,) * len(shape), pipeline_mode=pl.Buffered(1))


def twice(x):
    return jnp.concatenate([x, x], axis=1)


def qkv_kernel(tab, tok, sel, w, bq, bv, gain, shift, q_o, k_o, v_o):
    i = pl.program_id(0)
    needed = (i >= tab[12]) & (i <= tab[13])

    @pl.when(needed)
    def _():
        qkv_tile(tok, sel, w, bq, bv, gain, shift, q_o, k_o, v_o)

    @pl.when(jnp.logical_not(needed))
    def _():
        q_o[...] = jnp.zeros_like(q_o)
        k_o[...] = jnp.zeros_like(k_o)
        v_o[...] = jnp.zeros_like(v_o)


def qkv_tile(tok, sel, w, bq, bv, gain, shift, q_o, k_o, v_o):
    width = tok.shape[1]
    normal, _, _ = norm_forward(tok[...].astype(f32), gain[...], shift[...])
    n1 = normal.astype(bf16)
    select = sel[...]
    low = dot_nn(n1, w[:, 3 * width : 3 * width + 2 * LANES]).astype(bf16)
    low_q = low[:, :LANES] * select
    low_v = low[:, LANES:] * select
    q_out = w[:, 3 * width + 2 * LANES : 3 * width + 3 * LANES]
    v_out = w[:, 3 * width + 3 * LANES : 3 * width + 4 * LANES]
    scale = (width // HEADS) ** -0.5
    q = dot_nn(n1, w[:, :width]) + bq[...] + dot_nt(low_q, q_out)
    q_o[...] = (q * scale).astype(bf16)
    k_o[...] = dot_nn(n1, w[:, width : 2 * width]).astype(bf16)
    v = dot_nn(n1, w[:, 2 * width : 3 * width]) + bv[...] + dot_nt(low_v, v_out)
    v_o[...] = v.astype(bf16)


def qkv_call(tab, tok_w, sel_w, w_a, bq, bv, gain, shift):
    rows, width = tok_w.shape
    tile = pl.BlockSpec((TILE, width), lambda i, *_: (i, 0))
    vec = whole((1, width))
    out = jax.ShapeDtypeStruct((rows, width), bf16)
    return pl.pallas_call(
        qkv_kernel,
        grid_spec=pltpu.PrefetchScalarGridSpec(
            num_scalar_prefetch=1,
            grid=(rows // TILE,),
            in_specs=[
                tile,
                pl.BlockSpec((TILE, LANES), lambda i, *_: (i, 0)),
                whole((width, 3 * width + 4 * LANES)),
                vec,
                vec,
                vec,
                vec,
            ],
            out_specs=[tile] * 3,
        ),
        out_shape=[out] * 3,
        compiler_params=params(1),
        name="qkv",
    )(tab, tok_w, sel_w, w_a, bq, bv, gain, shift)


def head_masks(rows):
    lane = lax.broadcasted_iota(jnp.int32, (rows, LANES), 1)
    return lane < (LANES // 2)


def columns(c):
    return slice(c * LANES, (c + 1) * LANES)


def attend_kernel(tab, q, k, v, segc, segr, mixed_o, lse_o, s_scr):
    own = mixed_o.shape[0]
    wide = q.shape[1] // LANES
    first = head_masks(TILE)
    one = jnp.ones((), bf16)

    @pl.loop(0, own // TILE)
    def _(i):
        start, count = tab[2 * i], tab[2 * i + 1]
        row = pl.ds(pl.multiple_of(HALO + TILE * i, LANES), TILE)
        qs = [split_pair(q[row, columns(c)], first) for c in range(wide)]
        sq = twice(segc[row, :])

        def scores(t, carry):
            at = start + 2 * t
            here = pl.ds(pl.multiple_of(at * LANES, LANES), TILE)
            sk = jnp.concatenate([segr[pl.ds(at, 1), :], segr[pl.ds(at + 1, 1), :]], axis=1)
            mask = sq == sk
            out = []
            for c in range(wide):
                both = dot_nt(qs[c], k[here, columns(c)])
                for head in range(2):
                    x = jnp.where(mask, both[head * TILE : (head + 1) * TILE], NEG)
                    s_scr[2 * c + head, t] = x
                    out.append(
                        jnp.maximum(carry[2 * c + head], jnp.maximum(x[:, :LANES], x[:, LANES:]))
                    )
            return tuple(out)

        low = jnp.full((TILE, LANES), NEG, f32)
        tops = lax.fori_loop(0, count, scores, (low,) * (2 * wide))
        tops = [jnp.max(m, axis=1, keepdims=True) for m in tops]

        def weigh(t, carry):
            at = start + 2 * t
            here = pl.ds(pl.multiple_of(at * LANES, LANES), TILE)
            out = []
            for c in range(wide):
                vt = v[here, columns(c)]
                p0 = jnp.exp(s_scr[2 * c, t] - tops[2 * c]).astype(bf16)
                p1 = jnp.exp(s_scr[2 * c + 1, t] - tops[2 * c + 1]).astype(bf16)
                out.append(carry[2 * c] + dot_nn(p0, jnp.where(first, vt, one)))
                out.append(carry[2 * c + 1] + dot_nn(p1, jnp.where(first, one, vt)))
            return tuple(out)

        empty = jnp.zeros((TILE, LANES), f32)
        sums = lax.fori_loop(0, count, weigh, (empty,) * (2 * wide))
        for c in range(wide):
            a0, a1 = sums[2 * c], sums[2 * c + 1]
            r0 = pltpu.roll(a0, LANES // 2, 1)
            r1 = pltpu.roll(a1, LANES // 2, 1)
            out = jnp.where(first, a0 / r0, a1 / r1).astype(bf16)
            mixed_o[pl.ds(pl.multiple_of(TILE * i, TILE), TILE), columns(c)] = out
            l0 = (tops[2 * c] + jnp.log(jnp.where(first, r0, a0))).T
            l1 = (tops[2 * c + 1] + jnp.log(jnp.where(first, a1, r1))).T
            for half in range(2):
                at = 2 * i + half
                lse_o[c, 0, pl.ds(at, 1), :] = l0[0:1, columns(half)]
                lse_o[c, 1, pl.ds(at, 1), :] = l1[0:1, columns(half)]


def attend_call(tab, q, k, v, segc, segr, own):
    rows, width = q.shape
    pairs = width // LANES
    col = pl.BlockSpec((rows, WIDE * LANES), lambda h, *_: (0, h))
    return pl.pallas_call(
        attend_kernel,
        grid_spec=pltpu.PrefetchScalarGridSpec(
            num_scalar_prefetch=1,
            grid=(pairs // WIDE,),
            in_specs=[col, col, col, whole(segc.shape), whole(segr.shape)],
            out_specs=[
                pl.BlockSpec((own, WIDE * LANES), lambda h, *_: (0, h)),
                pl.BlockSpec((WIDE, 2, own // LANES, LANES), lambda h, *_: (h, 0, 0, 0)),
            ],
            scratch_shapes=[pltpu.VMEM((2 * WIDE, rows // TILE, TILE, TILE), f32)],
        ),
        out_shape=[
            jax.ShapeDtypeStruct((own, width), bf16),
            jax.ShapeDtypeStruct((pairs, 2, own // LANES, LANES), f32),
        ],
        compiler_params=params(1),
        name="attend",
    )(tab, q, k, v, segc, segr)


def split_pair(x, first):
    zero = jnp.zeros((), bf16)
    return jnp.concatenate([jnp.where(first, x, zero), jnp.where(first, zero, x)], axis=0)


def pair_grads(kt, vt, qcat, dcat, mask, lse0, lse1, dlt0, dlt1):
    half = qcat.shape[0] // 2
    s = dot_nt(kt, qcat)
    dp = dot_nt(vt, dcat)
    p0 = jnp.exp(jnp.where(mask, s[:, :half], NEG) - lse0)
    p1 = jnp.exp(jnp.where(mask, s[:, half:], NEG) - lse1)
    d0 = (p0 * (dp[:, :half] - dlt0)).astype(bf16)
    d1 = (p1 * (dp[:, half:] - dlt1)).astype(bf16)
    probs = jnp.concatenate([p0.astype(bf16), p1.astype(bf16)], axis=1)
    return probs, d0, d1


def attend_back_kernel(tab, q, k, v, dm, lse, dlt, segc, segr, dq_o, dk_o, dv_o, dk_a, dv_a):
    own = dm.shape[0]
    wide = q.shape[1] // LANES
    first = head_masks(TILE)
    scale = (LANES // 2) ** -0.5
    dk_a[...] = jnp.zeros_like(dk_a)
    dv_a[...] = jnp.zeros_like(dv_a)

    @pl.loop(0, own // TILE)
    def _(i):
        start, count = tab[2 * i], tab[2 * i + 1]
        row = pl.ds(pl.multiple_of(HALO + TILE * i, LANES), TILE)
        here = pl.ds(pl.multiple_of(TILE * i, TILE), TILE)
        qs = [split_pair(q[row, columns(c)], first) for c in range(wide)]
        ds = [split_pair(dm[here, columns(c)], first) for c in range(wide)]

        def line(ref, c, head):
            return jnp.concatenate(
                [ref[c, head, pl.ds(2 * i, 1), :], ref[c, head, pl.ds(2 * i + 1, 1), :]], axis=1
            )

        stats = [[line(ref, c, head) for ref in (lse, dlt) for head in range(2)] for c in range(wide)]
        at_q = HALO // LANES + 2 * i
        sq = jnp.concatenate([segr[pl.ds(at_q, 1), :], segr[pl.ds(at_q + 1, 1), :]], axis=1)

        def step(t, carry):
            at = pl.ds(pl.multiple_of((start + 2 * t) * LANES, LANES), TILE)
            mask = twice(segc[at, :]) == sq
            out = []
            for c in range(wide):
                kt = k[at, columns(c)]
                vt = v[at, columns(c)]
                probs, d0, d1 = pair_grads(kt, vt, qs[c], ds[c], mask, *stats[c])
                dv_a[at, columns(c)] += dot_nn(probs, ds[c])
                dk_a[at, columns(c)] += dot_nn(jnp.concatenate([d0, d1], axis=1), qs[c])
                out += [carry[2 * c] + dot_tn(d0, kt), carry[2 * c + 1] + dot_tn(d1, kt)]
            return tuple(out)

        empty = jnp.zeros((TILE, LANES), f32)
        sums = lax.fori_loop(0, count, step, (empty,) * (2 * wide))
        for c in range(wide):
            dq_o[here, columns(c)] = (
                jnp.where(first, sums[2 * c], sums[2 * c + 1]) * scale
            ).astype(bf16)

    dk_o[...] = dk_a[HALO : HALO + own, :]
    dv_o[...] = dv_a[HALO : HALO + own, :]


def attend_back_call(tab, q, k, v, dm, lse, dlt, segc, segr):
    rows, width = q.shape
    own = dm.shape[0]
    pairs = width // LANES
    col = pl.BlockSpec((rows, WIDE * LANES), lambda h, *_: (0, h))
    own_col = pl.BlockSpec((own, WIDE * LANES), lambda h, *_: (0, h))
    stat = pl.BlockSpec((WIDE, 2, own // LANES, LANES), lambda h, *_: (h, 0, 0, 0))
    return pl.pallas_call(
        attend_back_kernel,
        grid_spec=pltpu.PrefetchScalarGridSpec(
            num_scalar_prefetch=1,
            grid=(pairs // WIDE,),
            in_specs=[col, col, col, own_col, stat, stat, whole(segc.shape), whole(segr.shape)],
            out_specs=[own_col] * 3,
            scratch_shapes=[pltpu.VMEM((rows, WIDE * LANES), f32)] * 2,
        ),
        out_shape=[
            jax.ShapeDtypeStruct((own, width), bf16),
            jax.ShapeDtypeStruct((own, width), f32),
            jax.ShapeDtypeStruct((own, width), f32),
        ],
        compiler_params=params(1),
        name="attend_back",
    )(tab, q, k, v, dm, lse, dlt, segc, segr)


def halo_back_kernel(
    tab, q, k, v, dm_l, dm_r, st_l, st_r, dk_i, dv_i, segc, segr, dk_o, dv_o, dk_a, dv_a
):
    own = dk_o.shape[0]
    wide = q.shape[1] // LANES
    first = head_masks(LANES)
    dk_a[...] = dk_i[...]
    dv_a[...] = dv_i[...]
    for side in range(2):
        base = 6 + 3 * side
        count_q, k_first, count_k = tab[base], tab[base + 1], tab[base + 2]
        dm, st = (dm_l, st_l) if side == 0 else (dm_r, st_r)

        def query_tile(t, carry):
            tile = HALO // LANES - 1 - t if side == 0 else t
            tile_w = tile if side == 0 else tile + (HALO + own) // LANES
            at_h = pl.ds(pl.multiple_of(tile * LANES, LANES), LANES)
            at_w = pl.ds(pl.multiple_of(tile_w * LANES, LANES), LANES)
            qs = [split_pair(q[at_w, columns(c)], first) for c in range(wide)]
            ds = [split_pair(dm[at_h, columns(c)], first) for c in range(wide)]
            stats = [
                [st[kind, c, head, pl.ds(tile, 1), :] for kind in range(2) for head in range(2)]
                for c in range(wide)
            ]
            sq = segr[pl.ds(tile_w, 1), :]

            def key_tile(u, inner):
                at = pl.ds(pl.multiple_of((k_first + u) * TILE, TILE), TILE)
                at_k = pl.ds(pl.multiple_of(HALO + (k_first + u) * TILE, LANES), TILE)
                mask = segc[at_k, :] == sq
                for c in range(wide):
                    kt = k[at_k, columns(c)]
                    vt = v[at_k, columns(c)]
                    probs, d0, d1 = pair_grads(kt, vt, qs[c], ds[c], mask, *stats[c])
                    dv_a[at, columns(c)] += dot_nn(probs, ds[c])
                    dk_a[at, columns(c)] += dot_nn(jnp.concatenate([d0, d1], axis=1), qs[c])
                return inner

            return lax.fori_loop(0, count_k, key_tile, carry)

        lax.fori_loop(0, count_q, query_tile, 0)
    dk_o[...] = dk_a[...].astype(bf16)
    dv_o[...] = dv_a[...].astype(bf16)


def halo_back_call(tab, q, k, v, dm_l, dm_r, st_l, st_r, dk, dv, segc, segr):
    rows, width = q.shape
    own = dk.shape[0]
    pairs = width // LANES
    col = pl.BlockSpec((rows, WIDE * LANES), lambda h, *_: (0, h))
    own_col = pl.BlockSpec((own, WIDE * LANES), lambda h, *_: (0, h))
    halo_col = pl.BlockSpec((HALO, WIDE * LANES), lambda h, *_: (0, h))
    stat = pl.BlockSpec((2, WIDE, 2, HALO // LANES, LANES), lambda h, *_: (0, h, 0, 0, 0))
    return pl.pallas_call(
        halo_back_kernel,
        grid_spec=pltpu.PrefetchScalarGridSpec(
            num_scalar_prefetch=1,
            grid=(pairs // WIDE,),
            in_specs=[
                col,
                col,
                col,
                halo_col,
                halo_col,
                stat,
                stat,
                own_col,
                own_col,
                whole(segc.shape),
                whole(segr.shape),
            ],
            out_specs=[own_col] * 2,
            scratch_shapes=[pltpu.VMEM((own, WIDE * LANES), f32)] * 2,
        ),
        out_shape=[jax.ShapeDtypeStruct((own, width), bf16)] * 2,
        compiler_params=params(1),
        name="halo_back",
    )(tab, q, k, v, dm_l, dm_r, st_l, st_r, dk, dv, segc, segr)


FF_TILE = 512


def mlp_kernel(
    mixed, tok, dy, sel, w_out, w_up, w_lo, w_dn, w_x, b_out, b_up, b_down, gain, shift, heads,
    out_o, dres_o, dmix_o, head_o, tail_o, dlt_o, gui_o, gdo_o, guo_o, gdi_o,
    resid, n2, low_u, dlow_d, low_ut, dlow_dt, acc, acc_low, dn2, dlow_u, gdo_t, gui_t,
):
    j = pl.program_id(0)
    rows, width = mixed.shape
    chunks = [pl.ds(r, TILE) for r in range(0, rows, TILE)]
    up_in = w_lo[:, :LANES]
    down_out = w_lo[:, LANES:]
    out_w = w_out[...].reshape(width, width)

    @pl.when(j == 0)
    def _():
        for r in chunks:
            x = tok[r, :].astype(f32) + dot_nn(mixed[r, :], out_w) + b_out[...]
            resid[r, :] = x
            normal, _, _ = norm_forward(x, gain[...], shift[...])
            normal = normal.astype(bf16)
            n2[r, :] = normal
            lu = dot_nn(normal, up_in).astype(bf16) * sel[r, :]
            ld = dot_nn(dy[r, :], down_out).astype(bf16) * sel[r, :]
            low_u[r, :] = lu
            dlow_d[r, :] = ld
            low_ut[:, r] = lu.astype(f32).T.astype(bf16)
            dlow_dt[:, r] = ld.astype(f32).T.astype(bf16)
        acc[...] = jnp.zeros_like(acc)
        acc_low[...] = jnp.zeros_like(acc_low)
        dn2[...] = jnp.zeros_like(dn2)
        dlow_u[...] = jnp.zeros_like(dlow_u)
        gdo_t[...] = jnp.zeros_like(gdo_t)
        gui_t[...] = jnp.zeros_like(gui_t)

    down = w_dn[...].reshape(FF_TILE, width)
    up_w = w_up[...].reshape(width, FF_TILE)
    if len(w_x.shape) == 2:
        up_out, down_in = w_x[:, :LANES], w_x[:, LANES:]
    else:
        x = w_x[...]
        columns = [slice(c, c + LANES) for c in range(0, width, LANES)]
        half = len(columns) // 2
        up_out = jnp.concatenate([x[p, :, c] for p in range(x.shape[0]) for c in columns[:half]], axis=0)
        down_in = jnp.concatenate([x[p, :, c] for p in range(x.shape[0]) for c in columns[half:]], axis=0)
    guo_t = jnp.zeros((LANES, FF_TILE), f32)
    gdi_t = jnp.zeros((LANES, FF_TILE), f32)
    for r in chunks:
        pre = dot_nn(n2[r, :], up_w) + b_up[...] + dot_nt(low_u[r, :], up_out)
        d_act = dot_nt(dy[r, :], down) + dot_nt(dlow_d[r, :], down_in)
        gate = 1.0 / (1.0 + jnp.exp(-SLOPE * pre))
        act = pre * gate
        d_pre = (d_act * (gate + SLOPE * act * (1.0 - gate))).astype(bf16)
        act = act.astype(bf16)
        acc[r, :] += dot_nn(act, down)
        acc_low[r, :] += dot_nn(act, down_in)
        dn2[r, :] += dot_nt(d_pre, up_w)
        dlow_u[r, :] += dot_nn(d_pre, up_out)
        guo_t += dot_nn(low_ut[:, r], d_pre)
        gdi_t += dot_nn(dlow_dt[:, r], act)
    guo_o[...] = guo_t.T.astype(bf16)
    gdi_o[...] = gdi_t.T.astype(bf16)

    @pl.when(j == pl.num_programs(0) - 1)
    def _():
        for r in chunks:
            select = sel[r, :]
            x = resid[r, :]
            low_d = acc_low[r, :].astype(bf16) * select
            out_o[r, :] = (x + acc[r, :] + b_down[...] + dot_nt(low_d, down_out)).astype(bf16)
            lu = dlow_u[r, :].astype(bf16) * select
            _, hat, inv = norm_forward(x, gain[...], shift[...])
            grad = dn2[r, :] + dot_nt(lu, up_in)
            dres = dy[r, :].astype(f32) + norm_backward(grad, hat, inv, gain[...])
            dres_o[r, :] = dres
            dmix = dot_nt(dres.astype(bf16), out_w).astype(bf16)
            dmix_o[r, :] = dmix
            at = r.start
            upper = min(HALO - at, TILE)
            head_o[at : at + upper, :] = dmix[:upper]
            skip = max(rows - HALO - at, 0)
            first = at + skip - (rows - HALO)
            tail_o[first : first + TILE - skip, :] = dmix[skip:]
            prod = dmix.astype(f32) * mixed[r, :].astype(f32)
            high = prod.astype(bf16)
            rest = (prod - high.astype(f32)).astype(bf16)
            dlt_o[:, r] = dot_nt(heads[...], high) + dot_nt(heads[...], rest)
            gdo_t[...] += dot_nn(low_d.astype(f32).T.astype(bf16), dy[r, :])
            gui_t[...] += dot_nn(lu.astype(f32).T.astype(bf16), n2[r, :])
        gdo_o[...] = gdo_t[...].T.astype(bf16)
        gui_o[...] = gui_t[...].T.astype(bf16)


def mlp_call(mixed, tok, dy, sel, w_a, w_b, w_c, b_out, b_up, b_down, gain, shift, heads):
    rows, width = mixed.shape
    hidden = b_up.shape[1]
    full = whole((rows, width))
    vec = whole((1, width))
    low = whole((rows, LANES))
    at_low = (3 * width + 4 * LANES) // (2 * LANES)
    grads = jax.ShapeDtypeStruct((width, LANES), bf16)
    grads_ff = jax.ShapeDtypeStruct((hidden, LANES), bf16)
    const = lambda shape: pl.BlockSpec(shape, lambda j: (0,) * len(shape))
    once = pl.Buffered(1)
    ff_rows = pl.BlockSpec((FF_TILE, LANES), lambda j: (j, 0))
    if w_c is None:
        devices = w_b.shape[0]
        r, r_ff = width // devices, hidden // devices
        lead = (r_ff + r) // r
        per = width // FF_TILE
        at_x = lead + hidden // width
        group = FF_TILE // r_ff
        specs = [
            pl.BlockSpec((devices, r, width), lambda j: (0, r_ff // r, 0), pipeline_mode=once),
            pl.BlockSpec((devices, r, FF_TILE), lambda j: (0, lead + j // per, j % per)),
            pl.BlockSpec((group, r_ff, width), lambda j: (j, 0, 0)),
            pl.BlockSpec((group, r, width), lambda j: (j, at_x, 0)),
        ]
        weights = [w_b] * 4
    else:
        lead = width // FF_TILE
        specs = [
            whole((width, width)),
            pl.BlockSpec((width, FF_TILE), lambda j: (0, lead + j)),
            pl.BlockSpec((FF_TILE, width), lambda j: (j, 0)),
            pl.BlockSpec((FF_TILE, 2 * LANES), lambda j: (j, width // (2 * LANES))),
        ]
        weights = [w_b, w_b, w_c, w_c]
    return pl.pallas_call(
        mlp_kernel,
        grid=(hidden // FF_TILE,),
        in_specs=[
            full,
            full,
            full,
            low,
            specs[0],
            specs[1],
            pl.BlockSpec((width, 2 * LANES), lambda j: (0, at_low), pipeline_mode=once),
            specs[2],
            specs[3],
            vec,
            pl.BlockSpec((1, FF_TILE), lambda j: (0, j)),
            vec,
            vec,
            vec,
            whole(heads.shape),
        ],
        out_specs=[
            const((rows, width)),
            const((rows, width)),
            const((rows, width)),
            const((HALO, width)),
            const((HALO, width)),
            const((HEADS, rows)),
            const((width, LANES)),
            const((width, LANES)),
            ff_rows,
            ff_rows,
        ],
        out_shape=[
            jax.ShapeDtypeStruct((rows, width), bf16),
            jax.ShapeDtypeStruct((rows, width), f32),
            jax.ShapeDtypeStruct((rows, width), bf16),
            jax.ShapeDtypeStruct((HALO, width), bf16),
            jax.ShapeDtypeStruct((HALO, width), bf16),
            jax.ShapeDtypeStruct((HEADS, rows), f32),
            grads,
            grads,
            grads_ff,
            grads_ff,
        ],
        scratch_shapes=[
            pltpu.VMEM((rows, width), f32),
            pltpu.VMEM((rows, width), bf16),
            pltpu.VMEM((rows, LANES), bf16),
            pltpu.VMEM((rows, LANES), bf16),
            pltpu.VMEM((LANES, rows), bf16),
            pltpu.VMEM((LANES, rows), bf16),
            pltpu.VMEM((rows, width), f32),
            pltpu.VMEM((rows, LANES), f32),
            pltpu.VMEM((rows, width), f32),
            pltpu.VMEM((rows, LANES), f32),
            pltpu.VMEM((LANES, width), f32),
            pltpu.VMEM((LANES, width), f32),
        ],
        compiler_params=params(1),
        name="mlp",
    )(mixed, tok, dy, sel, weights[0], weights[1], w_a, weights[2], weights[3],
      b_out, b_up, b_down, gain, shift, heads)


def low_back_kernel(dq, dv, tok, sel, w, gain, shift, dlow_o, grads_o, acc):
    i = pl.program_id(0)
    normal, _, _ = norm_forward(tok[...].astype(f32), gain[...], shift[...])
    n1 = normal.astype(bf16)
    select = sel[...]
    low = dot_nn(n1, w[:, : 2 * LANES]).astype(bf16)
    low_q = low[:, :LANES] * select
    low_v = low[:, LANES:] * select
    dlow_q = dot_nn(dq[...], w[:, 2 * LANES : 3 * LANES]).astype(bf16) * select
    dlow_v = dot_nn(dv[...], w[:, 3 * LANES : 4 * LANES]).astype(bf16) * select
    dlow_o[:, :LANES] = dlow_q
    dlow_o[:, LANES:] = dlow_v

    @pl.when(i == 0)
    def _():
        acc[...] = jnp.zeros_like(acc)

    def turned(x):
        return x.astype(f32).T.astype(bf16)

    acc[0] += dot_nn(turned(dlow_q), n1)
    acc[1] += dot_nn(turned(low_q), dq[...])
    acc[2] += dot_nn(turned(dlow_v), n1)
    acc[3] += dot_nn(turned(low_v), dv[...])

    @pl.when(i == pl.num_programs(0) - 1)
    def _():
        for at in range(4):
            grads_o[at] = acc[at].T.astype(bf16)


def low_back_call(dq, dv, tok, sel, w_a, gain, shift):
    rows, width = tok.shape
    tile = pl.BlockSpec((TILE, width), lambda i: (i, 0))
    vec = whole((1, width))
    low = pl.BlockSpec((TILE, LANES), lambda i: (i, 0))
    at_low = 3 * width // (4 * LANES)
    return pl.pallas_call(
        low_back_kernel,
        grid=(rows // TILE,),
        in_specs=[
            tile,
            tile,
            tile,
            low,
            pl.BlockSpec((width, 4 * LANES), lambda i: (0, at_low), pipeline_mode=pl.Buffered(1)),
            vec,
            vec,
        ],
        out_specs=[
            pl.BlockSpec((TILE, 2 * LANES), lambda i: (i, 0)),
            pl.BlockSpec((4, width, LANES), lambda i: (0, 0, 0)),
        ],
        out_shape=[
            jax.ShapeDtypeStruct((rows, 2 * LANES), bf16),
            jax.ShapeDtypeStruct((4, width, LANES), bf16),
        ],
        scratch_shapes=[pltpu.VMEM((4, LANES, width), f32)],
        compiler_params=params(1),
        name="low_back",
    )(dq, dv, tok, sel, w_a, gain, shift)


def qkv_back_kernel(dq, dk, dv, dlow, tok, dres, w, gain, shift, gin_o):
    width = tok.shape[1]
    _, hat, inv = norm_forward(tok[...].astype(f32), gain[...], shift[...])
    grad = (
        dot_nt(dq[...], w[:, :width])
        + dot_nt(dk[...], w[:, width : 2 * width])
        + dot_nt(dv[...], w[:, 2 * width : 3 * width])
        + dot_nt(dlow[...], w[:, 3 * width : 3 * width + 2 * LANES])
    )
    gin_o[...] = (dres[...] + norm_backward(grad, hat, inv, gain[...])).astype(bf16)


def qkv_back_call(dq, dk, dv, dlow, tok, dres, w_a, gain, shift):
    rows, width = tok.shape
    tile = pl.BlockSpec((TILE, width), lambda i: (i, 0))
    vec = whole((1, width))
    return pl.pallas_call(
        qkv_back_kernel,
        grid=(rows // TILE,),
        in_specs=[
            tile,
            tile,
            tile,
            pl.BlockSpec((TILE, 2 * LANES), lambda i: (i, 0)),
            tile,
            tile,
            whole((width, 3 * width + 4 * LANES)),
            vec,
            vec,
        ],
        out_specs=tile,
        out_shape=jax.ShapeDtypeStruct((rows, width), bf16),
        compiler_params=params(1),
        name="qkv_back",
    )(dq, dk, dv, dlow, tok, dres, w_a, gain, shift)


def summed(parts, devices):
    packed = jnp.concatenate([p.reshape(devices, -1, p.shape[-1]) for p in parts], axis=1)
    got = lax.all_to_all(packed, AXES, 0, 0, tiled=True)
    return jnp.sum(got.astype(f32), axis=0)


def local(
    tokens, cotangent, segments, adapter_ids, ln1_gain, ln1_bias, w_query, b_query, w_key, w_value,
    b_value, w_out, b_out, ln2_gain, ln2_bias, w_up, b_up, w_down, b_down, query_in, query_out,
    value_in, value_out, up_in, up_out, down_in, down_out,
):
    own, width = tokens.shape
    inner = lax.axis_size("dp")
    devices = lax.axis_size("fsdp") * inner
    up = [(i, i + 1) for i in range(devices - 1)]
    down = [(i + 1, i) for i in range(devices - 1)]

    def gather(*pieces):
        return lax.all_gather(jnp.concatenate(pieces, axis=1), AXES, axis=0, tiled=True)

    before = lax.ppermute(tokens[own - HALO :], AXES, up)
    after = lax.ppermute(tokens[:HALO], AXES, down)
    w_a = gather(w_query, w_key, w_value, query_in, value_in, query_out, value_out, up_in, down_out)
    r, r_ff = w_out.shape[0], w_down.shape[0]
    if inner == 2 and r % 16 == 0 and 2 * LANES * (r_ff // r) == width:
        chunks = [slice(c, c + r) for c in range(0, r_ff, r)]
        low_maps = jnp.concatenate([m[c] for m in (up_out, down_in) for c in chunks], axis=1)
        up_blocks = [w_up[:, c : c + width] for c in range(0, w_up.shape[1], width)]
        mine = jnp.concatenate([w_down, w_out, *up_blocks, low_maps], axis=0)
        theirs = lax.ppermute(mine, "dp", [(0, 1), (1, 0)])
        is_first = lax.axis_index("dp") == 0
        both = jnp.stack([jnp.where(is_first, mine, theirs), jnp.where(is_first, theirs, mine)])
        w_b = lax.all_gather(both, "fsdp", axis=0, tiled=True)
        w_c = None
    else:
        w_b = gather(w_out, w_up)
        w_c = gather(w_down, up_out, down_in)

    position = lax.axis_index(AXES)
    padded = jnp.concatenate(
        [
            jnp.full((HALO,), -1, jnp.int32),
            segments,
            jnp.full((HALO,), 1 << 30, jnp.int32),
        ]
    )
    rows = own + 2 * HALO
    seg_w = lax.dynamic_slice_in_dim(padded, position * own, rows, 0)
    tile_seg = seg_w[HALO : HALO + own].reshape(own // TILE, TILE)
    images = jnp.concatenate([tile_seg[:, 0], tile_seg[:, -1]])
    low = jnp.sum((seg_w[None, :] < images[:, None]).astype(jnp.int32), axis=1)
    high = jnp.sum((seg_w[None, :] <= images[:, None]).astype(jnp.int32), axis=1)
    tiles = own // TILE
    entries = []
    for i in range(tiles):
        start = low[i] // LANES
        count = (high[tiles + i] - start * LANES + TILE - 1) // TILE
        entries += [jnp.minimum(start, rows // LANES - 2 * count), count]
    count_l = (HALO - low[0] + LANES - 1) // LANES
    entries += [
        jnp.maximum(count_l, 0),
        jnp.zeros((), jnp.int32),
        (jnp.minimum(high[0], HALO + own) - HALO + TILE - 1) // TILE,
    ]
    last = 2 * tiles - 1
    first_k = jnp.maximum(low[last] - HALO, 0) // TILE
    entries += [
        jnp.maximum((high[last] - HALO - own + LANES - 1) // LANES, 0),
        first_k,
        tiles - first_k,
        low[0] // TILE,
        (high[last] - 1) // TILE,
    ]
    tab = jnp.stack(entries)
    segr = seg_w.reshape(rows // LANES, LANES)
    segc = jnp.broadcast_to(seg_w[:, None], (rows, LANES))

    image_hot = (seg_w[:, None] == jnp.arange(adapter_ids.shape[0], dtype=jnp.int32)).astype(bf16)
    column = jnp.arange(ADAPTERS * RANK, dtype=jnp.int32) // RANK
    adapter_hot = (adapter_ids[:, None] == column[None, :]).astype(bf16)
    sel_w = dot_nn(image_hot, adapter_hot).astype(bf16)
    sel = sel_w[HALO : HALO + own]
    heads = (
        jnp.arange(width, dtype=jnp.int32)[None, :] // (width // HEADS)
        == jnp.arange(HEADS, dtype=jnp.int32)[:, None]
    ).astype(bf16)

    row = lambda x: x.reshape(1, -1)
    tok_w = jnp.concatenate([before, tokens, after], axis=0)
    q, k, v = qkv_call(
        tab, tok_w, sel_w, w_a, row(b_query), row(b_value), row(ln1_gain), row(ln1_bias)
    )
    mixed, lse = attend_call(tab, q, k, v, segc, segr, own)
    block_out, d_resid, d_mixed, dm_head, dm_tail, delta, g_ui, g_do, g_uo, g_di = mlp_call(
        mixed, tokens, cotangent, sel, w_a, w_b, w_c, row(b_out), row(b_up), row(b_down),
        row(ln2_gain), row(ln2_bias), heads,
    )
    dlt = delta.reshape(lse.shape)
    stats = jnp.stack([lse, dlt])
    cut = (own - HALO) // LANES
    dm_l = lax.ppermute(dm_tail, AXES, up)
    dm_r = lax.ppermute(dm_head, AXES, down)
    st_l = lax.ppermute(stats[:, :, :, cut:], AXES, up)
    st_r = lax.ppermute(stats[:, :, :, : HALO // LANES], AXES, down)
    mlp_grads = summed([g_ui, g_uo, g_di, g_do], devices)
    dq, dk, dv = attend_back_call(tab, q, k, v, d_mixed, lse, dlt, segc, segr)
    dk, dv = halo_back_call(tab, q, k, v, dm_l, dm_r, st_l, st_r, dk, dv, segc, segr)
    dlow, g_qv = low_back_call(dq, dv, tokens, sel, w_a, row(ln1_gain), row(ln1_bias))
    qv_grads = summed([g_qv[0], g_qv[1], g_qv[2], g_qv[3]], devices)
    grad_input = qkv_back_call(
        dq, dk, dv, dlow, tokens, d_resid, w_a, row(ln1_gain), row(ln1_bias)
    )
    return (
        block_out,
        grad_input,
        qv_grads[:r],
        qv_grads[r : 2 * r],
        qv_grads[2 * r : 3 * r],
        qv_grads[3 * r :],
        mlp_grads[:r],
        mlp_grads[r : r + r_ff],
        mlp_grads[r + r_ff : r + 2 * r_ff],
        mlp_grads[r + 2 * r_ff :],
    )


def solution(mesh):
    split = P(AXES, None)
    return jax.shard_map(
        local,
        mesh=mesh,
        in_specs=(
            split, split, P(), P(), P(), P(), split, P(), split, split, P(), split, P(), P(), P(),
            split, P(), split, P(), split, split, split, split, split, split, split, split,
        ),
        out_specs=(split,) * 10,
        check_vma=False,
    )
```

```python
import jax
import jax.numpy as jnp
from jax import lax
from jax.experimental import pallas as pl
from jax.experimental.pallas import tpu as pltpu
from jax.sharding import PartitionSpec as P


HEADS = 16
RANK = 16
ADAPTERS = 8
EPS = 1e-05
SLOPE = 1.702
NEG = -1000000000.0
AXES = ("fsdp", "dp")
LANES = 128
TILE = 256
HALO = 640
VMEM_LIMIT = 60 * 1024 * 1024
WIDE = 2

f32 = jnp.float32
bf16 = jnp.bfloat16


def dot_nn(a, b):
    return jnp.dot(a, b, preferred_element_type=f32)


def dot_nt(a, b):
    return lax.dot_general(a, b, (((1,), (1,)), ((), ())), preferred_element_type=f32)


def dot_tn(a, b):
    return lax.dot_general(a, b, (((0,), (0,)), ((), ())), preferred_element_type=f32)


def norm_forward(values, gain, shift):
    mean = jnp.mean(values, axis=1, keepdims=True)
    centered = values - mean
    inverse = lax.rsqrt(jnp.mean(centered * centered, axis=1, keepdims=True) + EPS)
    normed = centered * inverse
    return normed * gain + shift, normed, inverse


def norm_backward(grad, normed, inverse, gain):
    scaled = grad * gain
    return inverse * (
        scaled
        - jnp.mean(scaled, axis=1, keepdims=True)
        - normed * jnp.mean(scaled * normed, axis=1, keepdims=True)
    )


def params(grid_dims):
    return pltpu.CompilerParams(
        dimension_semantics=("arbitrary",) * grid_dims, vmem_limit_bytes=VMEM_LIMIT
    )


def whole(shape):
    return pl.BlockSpec(shape, lambda *_: (0,) * len(shape), pipeline_mode=pl.Buffered(1))


def twice(x):
    return jnp.concatenate([x, x], axis=1)


def qkv_kernel(tab, tok, sel, w, bq, bv, gain, shift, q_o, k_o, v_o):
    i = pl.program_id(0)
    needed = (i >= tab[12]) & (i <= tab[13])

    @pl.when(needed)
    def _():
        qkv_tile(tok, sel, w, bq, bv, gain, shift, q_o, k_o, v_o)

    @pl.when(jnp.logical_not(needed))
    def _():
        q_o[...] = jnp.zeros_like(q_o)
        k_o[...] = jnp.zeros_like(k_o)
        v_o[...] = jnp.zeros_like(v_o)


def qkv_tile(tok, sel, w, bq, bv, gain, shift, q_o, k_o, v_o):
    width = tok.shape[1]
    normal, _, _ = norm_forward(tok[...].astype(f32), gain[...], shift[...])
    n1 = normal.astype(bf16)
    select = sel[...]
    low = dot_nn(n1, w[:, 3 * width : 3 * width + 2 * LANES]).astype(bf16)
    low_q = low[:, :LANES] * select
    low_v = low[:, LANES:] * select
    q_out = w[:, 3 * width + 2 * LANES : 3 * width + 3 * LANES]
    v_out = w[:, 3 * width + 3 * LANES : 3 * width + 4 * LANES]
    scale = (width // HEADS) ** -0.5
    q = dot_nn(n1, w[:, :width]) + bq[...] + dot_nt(low_q, q_out)
    q_o[...] = (q * scale).astype(bf16)
    k_o[...] = dot_nn(n1, w[:, width : 2 * width]).astype(bf16)
    v = dot_nn(n1, w[:, 2 * width : 3 * width]) + bv[...] + dot_nt(low_v, v_out)
    v_o[...] = v.astype(bf16)


def qkv_call(tab, tok_w, sel_w, w_a, bq, bv, gain, shift):
    rows, width = tok_w.shape
    tile = pl.BlockSpec((TILE, width), lambda i, *_: (i, 0))
    vec = whole((1, width))
    out = jax.ShapeDtypeStruct((rows, width), bf16)
    return pl.pallas_call(
        qkv_kernel,
        grid_spec=pltpu.PrefetchScalarGridSpec(
            num_scalar_prefetch=1,
            grid=(rows // TILE,),
            in_specs=[
                tile,
                pl.BlockSpec((TILE, LANES), lambda i, *_: (i, 0)),
                whole((width, 3 * width + 4 * LANES)),
                vec,
                vec,
                vec,
                vec,
            ],
            out_specs=[tile] * 3,
        ),
        out_shape=[out] * 3,
        compiler_params=params(1),
        name="qkv",
    )(tab, tok_w, sel_w, w_a, bq, bv, gain, shift)


def head_masks(rows):
    lane = lax.broadcasted_iota(jnp.int32, (rows, LANES), 1)
    return lane < (LANES // 2)


def columns(c):
    return slice(c * LANES, (c + 1) * LANES)


def attend_kernel(tab, q, k, v, segc, segr, mixed_o, lse_o, s_scr):
    own = mixed_o.shape[0]
    wide = q.shape[1] // LANES
    first = head_masks(TILE)
    one = jnp.ones((), bf16)

    @pl.loop(0, own // TILE)
    def _(i):
        start, count = tab[2 * i], tab[2 * i + 1]
        row = pl.ds(pl.multiple_of(HALO + TILE * i, LANES), TILE)
        qs = [split_pair(q[row, columns(c)], first) for c in range(wide)]
        sq = twice(segc[row, :])

        def scores(t, carry):
            at = start + 2 * t
            here = pl.ds(pl.multiple_of(at * LANES, LANES), TILE)
            sk = jnp.concatenate([segr[pl.ds(at, 1), :], segr[pl.ds(at + 1, 1), :]], axis=1)
            mask = sq == sk
            out = []
            for c in range(wide):
                both = dot_nt(qs[c], k[here, columns(c)])
                for head in range(2):
                    x = jnp.where(mask, both[head * TILE : (head + 1) * TILE], NEG)
                    s_scr[2 * c + head, t] = x
                    out.append(
                        jnp.maximum(carry[2 * c + head], jnp.maximum(x[:, :LANES], x[:, LANES:]))
                    )
            return tuple(out)

        low = jnp.full((TILE, LANES), NEG, f32)
        tops = lax.fori_loop(0, count, scores, (low,) * (2 * wide))
        tops = [jnp.max(m, axis=1, keepdims=True) for m in tops]

        def weigh(t, carry):
            at = start + 2 * t
            here = pl.ds(pl.multiple_of(at * LANES, LANES), TILE)
            out = []
            for c in range(wide):
                vt = v[here, columns(c)]
                p0 = jnp.exp(s_scr[2 * c, t] - tops[2 * c]).astype(bf16)
                p1 = jnp.exp(s_scr[2 * c + 1, t] - tops[2 * c + 1]).astype(bf16)
                out.append(carry[2 * c] + dot_nn(p0, jnp.where(first, vt, one)))
                out.append(carry[2 * c + 1] + dot_nn(p1, jnp.where(first, one, vt)))
            return tuple(out)

        empty = jnp.zeros((TILE, LANES), f32)
        sums = lax.fori_loop(0, count, weigh, (empty,) * (2 * wide))
        for c in range(wide):
            a0, a1 = sums[2 * c], sums[2 * c + 1]
            r0 = pltpu.roll(a0, LANES // 2, 1)
            r1 = pltpu.roll(a1, LANES // 2, 1)
            out = jnp.where(first, a0 / r0, a1 / r1).astype(bf16)
            mixed_o[pl.ds(pl.multiple_of(TILE * i, TILE), TILE), columns(c)] = out
            l0 = (tops[2 * c] + jnp.log(jnp.where(first, r0, a0))).T
            l1 = (tops[2 * c + 1] + jnp.log(jnp.where(first, a1, r1))).T
            for half in range(2):
                at = 2 * i + half
                lse_o[c, 0, pl.ds(at, 1), :] = l0[0:1, columns(half)]
                lse_o[c, 1, pl.ds(at, 1), :] = l1[0:1, columns(half)]


def attend_call(tab, q, k, v, segc, segr, own):
    rows, width = q.shape
    pairs = width // LANES
    col = pl.BlockSpec((rows, WIDE * LANES), lambda h, *_: (0, h))
    return pl.pallas_call(
        attend_kernel,
        grid_spec=pltpu.PrefetchScalarGridSpec(
            num_scalar_prefetch=1,
            grid=(pairs // WIDE,),
            in_specs=[col, col, col, whole(segc.shape), whole(segr.shape)],
            out_specs=[
                pl.BlockSpec((own, WIDE * LANES), lambda h, *_: (0, h)),
                pl.BlockSpec((WIDE, 2, own // LANES, LANES), lambda h, *_: (h, 0, 0, 0)),
            ],
            scratch_shapes=[pltpu.VMEM((2 * WIDE, rows // TILE, TILE, TILE), f32)],
        ),
        out_shape=[
            jax.ShapeDtypeStruct((own, width), bf16),
            jax.ShapeDtypeStruct((pairs, 2, own // LANES, LANES), f32),
        ],
        compiler_params=params(1),
        name="attend",
    )(tab, q, k, v, segc, segr)


def split_pair(x, first):
    zero = jnp.zeros((), bf16)
    return jnp.concatenate([jnp.where(first, x, zero), jnp.where(first, zero, x)], axis=0)


def pair_grads(kt, vt, qcat, dcat, mask, lse0, lse1, dlt0, dlt1):
    half = qcat.shape[0] // 2
    s = dot_nt(kt, qcat)
    dp = dot_nt(vt, dcat)
    p0 = jnp.exp(jnp.where(mask, s[:, :half], NEG) - lse0)
    p1 = jnp.exp(jnp.where(mask, s[:, half:], NEG) - lse1)
    d0 = (p0 * (dp[:, :half] - dlt0)).astype(bf16)
    d1 = (p1 * (dp[:, half:] - dlt1)).astype(bf16)
    probs = jnp.concatenate([p0.astype(bf16), p1.astype(bf16)], axis=1)
    return probs, d0, d1


def attend_back_kernel(tab, q, k, v, dm, lse, dlt, segc, segr, dq_o, dk_o, dv_o, dk_a, dv_a):
    own = dm.shape[0]
    wide = q.shape[1] // LANES
    first = head_masks(TILE)
    scale = (LANES // 2) ** -0.5
    dk_a[...] = jnp.zeros_like(dk_a)
    dv_a[...] = jnp.zeros_like(dv_a)

    @pl.loop(0, own // TILE)
    def _(i):
        start, count = tab[2 * i], tab[2 * i + 1]
        row = pl.ds(pl.multiple_of(HALO + TILE * i, LANES), TILE)
        here = pl.ds(pl.multiple_of(TILE * i, TILE), TILE)
        qs = [split_pair(q[row, columns(c)], first) for c in range(wide)]
        ds = [split_pair(dm[here, columns(c)], first) for c in range(wide)]

        def line(ref, c, head):
            return jnp.concatenate(
                [ref[c, head, pl.ds(2 * i, 1), :], ref[c, head, pl.ds(2 * i + 1, 1), :]], axis=1
            )

        stats = [[line(ref, c, head) for ref in (lse, dlt) for head in range(2)] for c in range(wide)]
        at_q = HALO // LANES + 2 * i
        sq = jnp.concatenate([segr[pl.ds(at_q, 1), :], segr[pl.ds(at_q + 1, 1), :]], axis=1)

        def step(t, carry):
            at = pl.ds(pl.multiple_of((start + 2 * t) * LANES, LANES), TILE)
            mask = twice(segc[at, :]) == sq
            out = []
            for c in range(wide):
                kt = k[at, columns(c)]
                vt = v[at, columns(c)]
                probs, d0, d1 = pair_grads(kt, vt, qs[c], ds[c], mask, *stats[c])
                dv_a[at, columns(c)] += dot_nn(probs, ds[c])
                dk_a[at, columns(c)] += dot_nn(jnp.concatenate([d0, d1], axis=1), qs[c])
                out += [carry[2 * c] + dot_tn(d0, kt), carry[2 * c + 1] + dot_tn(d1, kt)]
            return tuple(out)

        empty = jnp.zeros((TILE, LANES), f32)
        sums = lax.fori_loop(0, count, step, (empty,) * (2 * wide))
        for c in range(wide):
            dq_o[here, columns(c)] = (
                jnp.where(first, sums[2 * c], sums[2 * c + 1]) * scale
            ).astype(bf16)

    dk_o[...] = dk_a[HALO : HALO + own, :]
    dv_o[...] = dv_a[HALO : HALO + own, :]


def attend_back_call(tab, q, k, v, dm, lse, dlt, segc, segr):
    rows, width = q.shape
    own = dm.shape[0]
    pairs = width // LANES
    col = pl.BlockSpec((rows, WIDE * LANES), lambda h, *_: (0, h))
    own_col = pl.BlockSpec((own, WIDE * LANES), lambda h, *_: (0, h))
    stat = pl.BlockSpec((WIDE, 2, own // LANES, LANES), lambda h, *_: (h, 0, 0, 0))
    return pl.pallas_call(
        attend_back_kernel,
        grid_spec=pltpu.PrefetchScalarGridSpec(
            num_scalar_prefetch=1,
            grid=(pairs // WIDE,),
            in_specs=[col, col, col, own_col, stat, stat, whole(segc.shape), whole(segr.shape)],
            out_specs=[own_col] * 3,
            scratch_shapes=[pltpu.VMEM((rows, WIDE * LANES), f32)] * 2,
        ),
        out_shape=[
            jax.ShapeDtypeStruct((own, width), bf16),
            jax.ShapeDtypeStruct((own, width), f32),
            jax.ShapeDtypeStruct((own, width), f32),
        ],
        compiler_params=params(1),
        name="attend_back",
    )(tab, q, k, v, dm, lse, dlt, segc, segr)


def halo_back_kernel(
    tab, q, k, v, dm_l, dm_r, st_l, st_r, dk_i, dv_i, segc, segr, dk_o, dv_o, dk_a, dv_a
):
    own = dk_o.shape[0]
    wide = q.shape[1] // LANES
    first = head_masks(LANES)
    dk_a[...] = dk_i[...]
    dv_a[...] = dv_i[...]
    for side in range(2):
        base = 6 + 3 * side
        count_q, k_first, count_k = tab[base], tab[base + 1], tab[base + 2]
        dm, st = (dm_l, st_l) if side == 0 else (dm_r, st_r)

        def query_tile(t, carry):
            tile = HALO // LANES - 1 - t if side == 0 else t
            tile_w = tile if side == 0 else tile + (HALO + own) // LANES
            at_h = pl.ds(pl.multiple_of(tile * LANES, LANES), LANES)
            at_w = pl.ds(pl.multiple_of(tile_w * LANES, LANES), LANES)
            qs = [split_pair(q[at_w, columns(c)], first) for c in range(wide)]
            ds = [split_pair(dm[at_h, columns(c)], first) for c in range(wide)]
            stats = [
                [st[kind, c, head, pl.ds(tile, 1), :] for kind in range(2) for head in range(2)]
                for c in range(wide)
            ]
            sq = segr[pl.ds(tile_w, 1), :]

            def key_tile(u, inner):
                at = pl.ds(pl.multiple_of((k_first + u) * TILE, TILE), TILE)
                at_k = pl.ds(pl.multiple_of(HALO + (k_first + u) * TILE, LANES), TILE)
                mask = segc[at_k, :] == sq
                for c in range(wide):
                    kt = k[at_k, columns(c)]
                    vt = v[at_k, columns(c)]
                    probs, d0, d1 = pair_grads(kt, vt, qs[c], ds[c], mask, *stats[c])
                    dv_a[at, columns(c)] += dot_nn(probs, ds[c])
                    dk_a[at, columns(c)] += dot_nn(jnp.concatenate([d0, d1], axis=1), qs[c])
                return inner

            return lax.fori_loop(0, count_k, key_tile, carry)

        lax.fori_loop(0, count_q, query_tile, 0)
    dk_o[...] = dk_a[...].astype(bf16)
    dv_o[...] = dv_a[...].astype(bf16)


def halo_back_call(tab, q, k, v, dm_l, dm_r, st_l, st_r, dk, dv, segc, segr):
    rows, width = q.shape
    own = dk.shape[0]
    pairs = width // LANES
    col = pl.BlockSpec((rows, WIDE * LANES), lambda h, *_: (0, h))
    own_col = pl.BlockSpec((own, WIDE * LANES), lambda h, *_: (0, h))
    halo_col = pl.BlockSpec((HALO, WIDE * LANES), lambda h, *_: (0, h))
    stat = pl.BlockSpec((2, WIDE, 2, HALO // LANES, LANES), lambda h, *_: (0, h, 0, 0, 0))
    return pl.pallas_call(
        halo_back_kernel,
        grid_spec=pltpu.PrefetchScalarGridSpec(
            num_scalar_prefetch=1,
            grid=(pairs // WIDE,),
            in_specs=[
                col,
                col,
                col,
                halo_col,
                halo_col,
                stat,
                stat,
                own_col,
                own_col,
                whole(segc.shape),
                whole(segr.shape),
            ],
            out_specs=[own_col] * 2,
            scratch_shapes=[pltpu.VMEM((own, WIDE * LANES), f32)] * 2,
        ),
        out_shape=[jax.ShapeDtypeStruct((own, width), bf16)] * 2,
        compiler_params=params(1),
        name="halo_back",
    )(tab, q, k, v, dm_l, dm_r, st_l, st_r, dk, dv, segc, segr)


FF_TILE = 512


def mlp_kernel(
    mixed, tok, dy, sel, w_out, w_up, w_lo, w_dn, w_x, b_out, b_up, b_down, gain, shift, heads,
    out_o, dres_o, dmix_o, head_o, tail_o, dlt_o, grads_o,
    resid, n2, low_u, dlow_d, low_ut, dlow_dt, acc, acc_low, dn2, dlow_u, gdo_t, gui_t,
):
    j = pl.program_id(0)
    rows, width = mixed.shape
    chunks = [pl.ds(r, TILE) for r in range(0, rows, TILE)]
    up_in = w_lo[:, :LANES]
    down_out = w_lo[:, LANES:]
    out_w = w_out[...].reshape(width, width)

    @pl.when(j == 0)
    def _():
        for r in chunks:
            x = tok[r, :].astype(f32) + dot_nn(mixed[r, :], out_w) + b_out[...]
            resid[r, :] = x
            normal, _, _ = norm_forward(x, gain[...], shift[...])
            normal = normal.astype(bf16)
            n2[r, :] = normal
            lu = dot_nn(normal, up_in).astype(bf16) * sel[r, :]
            ld = dot_nn(dy[r, :], down_out).astype(bf16) * sel[r, :]
            low_u[r, :] = lu
            dlow_d[r, :] = ld
            low_ut[:, r] = lu.astype(f32).T.astype(bf16)
            dlow_dt[:, r] = ld.astype(f32).T.astype(bf16)
        acc[...] = jnp.zeros_like(acc)
        acc_low[...] = jnp.zeros_like(acc_low)
        dn2[...] = jnp.zeros_like(dn2)
        dlow_u[...] = jnp.zeros_like(dlow_u)
        gdo_t[...] = jnp.zeros_like(gdo_t)
        gui_t[...] = jnp.zeros_like(gui_t)

    down = w_dn[...].reshape(FF_TILE, width)
    up_w = w_up[...].reshape(width, FF_TILE)
    if len(w_x.shape) == 2:
        up_out, down_in = w_x[:, :LANES], w_x[:, LANES:]
    else:
        x = w_x[...]
        columns = [slice(c, c + LANES) for c in range(0, width, LANES)]
        half = len(columns) // 2
        up_out = jnp.concatenate([x[p, :, c] for p in range(x.shape[0]) for c in columns[:half]], axis=0)
        down_in = jnp.concatenate([x[p, :, c] for p in range(x.shape[0]) for c in columns[half:]], axis=0)
    guo_t = jnp.zeros((LANES, FF_TILE), f32)
    gdi_t = jnp.zeros((LANES, FF_TILE), f32)
    for r in chunks:
        pre = dot_nn(n2[r, :], up_w) + b_up[...] + dot_nt(low_u[r, :], up_out)
        d_act = dot_nt(dy[r, :], down) + dot_nt(dlow_d[r, :], down_in)
        gate = 1.0 / (1.0 + jnp.exp(-SLOPE * pre))
        act = pre * gate
        d_pre = (d_act * (gate + SLOPE * act * (1.0 - gate))).astype(bf16)
        act = act.astype(bf16)
        acc[r, :] += dot_nn(act, down)
        acc_low[r, :] += dot_nn(act, down_in)
        dn2[r, :] += dot_nt(d_pre, up_w)
        dlow_u[r, :] += dot_nn(d_pre, up_out)
        guo_t += dot_nn(low_ut[:, r], d_pre)
        gdi_t += dot_nn(dlow_dt[:, r], act)
    owners, packed = grads_o.shape[:2]
    narrow = width // owners
    deep = packed // 2 - narrow
    group = FF_TILE // deep
    own_j = pl.ds(j * group, group)
    grads_o[own_j, 2 * narrow : 2 * narrow + deep, :] = guo_t.T.reshape(group, deep, LANES)
    grads_o[own_j, 2 * narrow + deep :, :] = gdi_t.T.reshape(group, deep, LANES)

    @pl.when(j == pl.num_programs(0) - 1)
    def _():
        for r in chunks:
            select = sel[r, :]
            x = resid[r, :]
            low_d = acc_low[r, :].astype(bf16) * select
            out_o[r, :] = (x + acc[r, :] + b_down[...] + dot_nt(low_d, down_out)).astype(bf16)
            lu = dlow_u[r, :].astype(bf16) * select
            _, hat, inv = norm_forward(x, gain[...], shift[...])
            grad = dn2[r, :] + dot_nt(lu, up_in)
            dres = dy[r, :].astype(f32) + norm_backward(grad, hat, inv, gain[...])
            dres_o[r, :] = dres
            dmix = dot_nt(dres.astype(bf16), out_w).astype(bf16)
            dmix_o[r, :] = dmix
            at = r.start
            upper = min(HALO - at, TILE)
            head_o[at : at + upper, :] = dmix[:upper]
            skip = max(rows - HALO - at, 0)
            first = at + skip - (rows - HALO)
            tail_o[first : first + TILE - skip, :] = dmix[skip:]
            prod = dmix.astype(f32) * mixed[r, :].astype(f32)
            high = prod.astype(bf16)
            rest = (prod - high.astype(f32)).astype(bf16)
            delta = dot_nt(heads[...], high) + dot_nt(heads[...], rest)
            for part in range(TILE // LANES):
                dlt_o[:, at // LANES + part, :] = delta[:, part * LANES : (part + 1) * LANES]
            gdo_t[...] += dot_nn(low_d.astype(f32).T.astype(bf16), dy[r, :])
            gui_t[...] += dot_nn(lu.astype(f32).T.astype(bf16), n2[r, :])
        grads_o[:, :narrow, :] = gui_t[...].T.reshape(owners, narrow, LANES)
        grads_o[:, narrow : 2 * narrow, :] = gdo_t[...].T.reshape(owners, narrow, LANES)


def mlp_call(mixed, tok, dy, sel, w_a, w_b, w_c, b_out, b_up, b_down, gain, shift, heads, owners):
    rows, width = mixed.shape
    hidden = b_up.shape[1]
    full = whole((rows, width))
    vec = whole((1, width))
    low = whole((rows, LANES))
    at_low = (3 * width + 4 * LANES) // (2 * LANES)
    packed = (owners, 2 * (width + hidden) // owners, LANES)
    const = lambda shape: pl.BlockSpec(shape, lambda j: (0,) * len(shape))
    once = pl.Buffered(1)
    if w_c is None:
        devices = w_b.shape[0]
        r, r_ff = width // devices, hidden // devices
        lead = (r_ff + r) // r
        per = width // FF_TILE
        at_x = lead + hidden // width
        group = FF_TILE // r_ff
        specs = [
            pl.BlockSpec((devices, r, width), lambda j: (0, r_ff // r, 0), pipeline_mode=once),
            pl.BlockSpec((devices, r, FF_TILE), lambda j: (0, lead + j // per, j % per)),
            pl.BlockSpec((group, r_ff, width), lambda j: (j, 0, 0)),
            pl.BlockSpec((group, r, width), lambda j: (j, at_x, 0)),
        ]
        weights = [w_b] * 4
    else:
        lead = width // FF_TILE
        specs = [
            whole((width, width)),
            pl.BlockSpec((width, FF_TILE), lambda j: (0, lead + j)),
            pl.BlockSpec((FF_TILE, width), lambda j: (j, 0)),
            pl.BlockSpec((FF_TILE, 2 * LANES), lambda j: (j, width // (2 * LANES))),
        ]
        weights = [w_b, w_b, w_c, w_c]
    return pl.pallas_call(
        mlp_kernel,
        grid=(hidden // FF_TILE,),
        in_specs=[
            full,
            full,
            full,
            low,
            specs[0],
            specs[1],
            pl.BlockSpec((width, 2 * LANES), lambda j: (0, at_low), pipeline_mode=once),
            specs[2],
            specs[3],
            vec,
            pl.BlockSpec((1, FF_TILE), lambda j: (0, j)),
            vec,
            vec,
            vec,
            whole(heads.shape),
        ],
        out_specs=[
            const((rows, width)),
            const((rows, width)),
            const((rows, width)),
            const((HALO, width)),
            const((HALO, width)),
            const((HEADS, rows // LANES, LANES)),
            const(packed),
        ],
        out_shape=[
            jax.ShapeDtypeStruct((rows, width), bf16),
            jax.ShapeDtypeStruct((rows, width), f32),
            jax.ShapeDtypeStruct((rows, width), bf16),
            jax.ShapeDtypeStruct((HALO, width), bf16),
            jax.ShapeDtypeStruct((HALO, width), bf16),
            jax.ShapeDtypeStruct((HEADS, rows // LANES, LANES), f32),
            jax.ShapeDtypeStruct(packed, f32),
        ],
        scratch_shapes=[
            pltpu.VMEM((rows, width), f32),
            pltpu.VMEM((rows, width), bf16),
            pltpu.VMEM((rows, LANES), bf16),
            pltpu.VMEM((rows, LANES), bf16),
            pltpu.VMEM((LANES, rows), bf16),
            pltpu.VMEM((LANES, rows), bf16),
            pltpu.VMEM((rows, width), f32),
            pltpu.VMEM((rows, LANES), f32),
            pltpu.VMEM((rows, width), f32),
            pltpu.VMEM((rows, LANES), f32),
            pltpu.VMEM((LANES, width), f32),
            pltpu.VMEM((LANES, width), f32),
        ],
        compiler_params=params(1),
        name="mlp",
    )(mixed, tok, dy, sel, weights[0], weights[1], w_a, weights[2], weights[3],
      b_out, b_up, b_down, gain, shift, heads)


def low_back_kernel(dq, dv, tok, sel, w, gain, shift, dlow_o, grads_o, acc):
    i = pl.program_id(0)
    normal, _, _ = norm_forward(tok[...].astype(f32), gain[...], shift[...])
    n1 = normal.astype(bf16)
    select = sel[...]
    low = dot_nn(n1, w[:, : 2 * LANES]).astype(bf16)
    low_q = low[:, :LANES] * select
    low_v = low[:, LANES:] * select
    dlow_q = dot_nn(dq[...], w[:, 2 * LANES : 3 * LANES]).astype(bf16) * select
    dlow_v = dot_nn(dv[...], w[:, 3 * LANES : 4 * LANES]).astype(bf16) * select
    dlow_o[:, :LANES] = dlow_q
    dlow_o[:, LANES:] = dlow_v

    @pl.when(i == 0)
    def _():
        acc[...] = jnp.zeros_like(acc)

    def turned(x):
        return x.astype(f32).T.astype(bf16)

    acc[0] += dot_nn(turned(dlow_q), n1)
    acc[1] += dot_nn(turned(low_q), dq[...])
    acc[2] += dot_nn(turned(dlow_v), n1)
    acc[3] += dot_nn(turned(low_v), dv[...])

    @pl.when(i == pl.num_programs(0) - 1)
    def _():
        for at in range(4):
            grads_o[at] = acc[at].T.astype(bf16)


def low_back_call(dq, dv, tok, sel, w_a, gain, shift):
    rows, width = tok.shape
    tile = pl.BlockSpec((TILE, width), lambda i: (i, 0))
    vec = whole((1, width))
    low = pl.BlockSpec((TILE, LANES), lambda i: (i, 0))
    at_low = 3 * width // (4 * LANES)
    return pl.pallas_call(
        low_back_kernel,
        grid=(rows // TILE,),
        in_specs=[
            tile,
            tile,
            tile,
            low,
            pl.BlockSpec((width, 4 * LANES), lambda i: (0, at_low), pipeline_mode=pl.Buffered(1)),
            vec,
            vec,
        ],
        out_specs=[
            pl.BlockSpec((TILE, 2 * LANES), lambda i: (i, 0)),
            pl.BlockSpec((4, width, LANES), lambda i: (0, 0, 0)),
        ],
        out_shape=[
            jax.ShapeDtypeStruct((rows, 2 * LANES), bf16),
            jax.ShapeDtypeStruct((4, width, LANES), bf16),
        ],
        scratch_shapes=[pltpu.VMEM((4, LANES, width), f32)],
        compiler_params=params(1),
        name="low_back",
    )(dq, dv, tok, sel, w_a, gain, shift)


def qkv_back_kernel(dq, dk, dv, dlow, tok, dres, w, gain, shift, gin_o):
    width = tok.shape[1]
    _, hat, inv = norm_forward(tok[...].astype(f32), gain[...], shift[...])
    grad = (
        dot_nt(dq[...], w[:, :width])
        + dot_nt(dk[...], w[:, width : 2 * width])
        + dot_nt(dv[...], w[:, 2 * width : 3 * width])
        + dot_nt(dlow[...], w[:, 3 * width : 3 * width + 2 * LANES])
    )
    gin_o[...] = (dres[...] + norm_backward(grad, hat, inv, gain[...])).astype(bf16)


def qkv_back_call(dq, dk, dv, dlow, tok, dres, w_a, gain, shift):
    rows, width = tok.shape
    tile = pl.BlockSpec((TILE, width), lambda i: (i, 0))
    vec = whole((1, width))
    return pl.pallas_call(
        qkv_back_kernel,
        grid=(rows // TILE,),
        in_specs=[
            tile,
            tile,
            tile,
            pl.BlockSpec((TILE, 2 * LANES), lambda i: (i, 0)),
            tile,
            tile,
            whole((width, 3 * width + 4 * LANES)),
            vec,
            vec,
        ],
        out_specs=tile,
        out_shape=jax.ShapeDtypeStruct((rows, width), bf16),
        compiler_params=params(1),
        name="qkv_back",
    )(dq, dk, dv, dlow, tok, dres, w_a, gain, shift)


def summed(parts, devices):
    packed = jnp.concatenate([p.reshape(devices, -1, p.shape[-1]) for p in parts], axis=1)
    got = lax.all_to_all(packed, AXES, 0, 0, tiled=True)
    return jnp.sum(got.astype(f32), axis=0)


def local(
    tokens, cotangent, segments, adapter_ids, ln1_gain, ln1_bias, w_query, b_query, w_key, w_value,
    b_value, w_out, b_out, ln2_gain, ln2_bias, w_up, b_up, w_down, b_down, query_in, query_out,
    value_in, value_out, up_in, up_out, down_in, down_out,
):
    own, width = tokens.shape
    inner = lax.axis_size("dp")
    devices = lax.axis_size("fsdp") * inner
    up = [(i, i + 1) for i in range(devices - 1)]
    down = [(i + 1, i) for i in range(devices - 1)]

    def gather(*pieces):
        return lax.all_gather(jnp.concatenate(pieces, axis=1), AXES, axis=0, tiled=True)

    before = lax.ppermute(tokens[own - HALO :], AXES, up)
    after = lax.ppermute(tokens[:HALO], AXES, down)
    first_maps = (w_query, w_key, w_value, query_in, value_in, query_out, value_out, up_in, down_out)
    r, r_ff = w_out.shape[0], w_down.shape[0]
    if inner == 2 and r % 16 == 0 and 2 * LANES * (r_ff // r) == width:
        chunks = [slice(c, c + r) for c in range(0, r_ff, r)]
        low_maps = jnp.concatenate([m[c] for m in (up_out, down_in) for c in chunks], axis=1)
        up_blocks = [w_up[:, c : c + width] for c in range(0, w_up.shape[1], width)]
        is_first = lax.axis_index("dp") == 0

        def gather_twice(mine):
            theirs = lax.ppermute(mine, "dp", [(0, 1), (1, 0)])
            both = jnp.stack([jnp.where(is_first, mine, theirs), jnp.where(is_first, theirs, mine)])
            return lax.all_gather(both, "fsdp", axis=0, tiled=True)

        w_a = gather_twice(jnp.concatenate(first_maps, axis=1)).reshape(r * devices, -1)
        w_b = gather_twice(jnp.concatenate([w_down, w_out, *up_blocks, low_maps], axis=0))
        w_c = None
    else:
        w_a = gather(*first_maps)
        w_b = gather(w_out, w_up)
        w_c = gather(w_down, up_out, down_in)

    position = lax.axis_index(AXES)
    padded = jnp.concatenate(
        [
            jnp.full((HALO,), -1, jnp.int32),
            segments,
            jnp.full((HALO,), 1 << 30, jnp.int32),
        ]
    )
    rows = own + 2 * HALO
    seg_w = lax.dynamic_slice_in_dim(padded, position * own, rows, 0)
    tile_seg = seg_w[HALO : HALO + own].reshape(own // TILE, TILE)
    images = jnp.concatenate([tile_seg[:, 0], tile_seg[:, -1]])
    low = jnp.sum((seg_w[None, :] < images[:, None]).astype(jnp.int32), axis=1)
    high = jnp.sum((seg_w[None, :] <= images[:, None]).astype(jnp.int32), axis=1)
    tiles = own // TILE
    entries = []
    for i in range(tiles):
        start = low[i] // LANES
        count = (high[tiles + i] - start * LANES + TILE - 1) // TILE
        entries += [jnp.minimum(start, rows // LANES - 2 * count), count]
    count_l = (HALO - low[0] + LANES - 1) // LANES
    entries += [
        jnp.maximum(count_l, 0),
        jnp.zeros((), jnp.int32),
        (jnp.minimum(high[0], HALO + own) - HALO + TILE - 1) // TILE,
    ]
    last = 2 * tiles - 1
    first_k = jnp.maximum(low[last] - HALO, 0) // TILE
    entries += [
        jnp.maximum((high[last] - HALO - own + LANES - 1) // LANES, 0),
        first_k,
        tiles - first_k,
        low[0] // TILE,
        (high[last] - 1) // TILE,
    ]
    tab = jnp.stack(entries)
    segr = seg_w.reshape(rows // LANES, LANES)
    segc = jnp.broadcast_to(seg_w[:, None], (rows, LANES))

    image_hot = (seg_w[:, None] == jnp.arange(adapter_ids.shape[0], dtype=jnp.int32)).astype(bf16)
    column = jnp.arange(ADAPTERS * RANK, dtype=jnp.int32) // RANK
    adapter_hot = (adapter_ids[:, None] == column[None, :]).astype(bf16)
    sel_w = dot_nn(image_hot, adapter_hot).astype(bf16)
    sel = sel_w[HALO : HALO + own]
    heads = (
        jnp.arange(width, dtype=jnp.int32)[None, :] // (width // HEADS)
        == jnp.arange(HEADS, dtype=jnp.int32)[:, None]
    ).astype(bf16)

    row = lambda x: x.reshape(1, -1)
    tok_w = jnp.concatenate([before, tokens, after], axis=0)
    q, k, v = qkv_call(
        tab, tok_w, sel_w, w_a, row(b_query), row(b_value), row(ln1_gain), row(ln1_bias)
    )
    mixed, lse = attend_call(tab, q, k, v, segc, segr, own)
    block_out, d_resid, d_mixed, dm_head, dm_tail, delta, g_ff = mlp_call(
        mixed, tokens, cotangent, sel, w_a, w_b, w_c, row(b_out), row(b_up), row(b_down),
        row(ln2_gain), row(ln2_bias), heads, devices // inner,
    )
    dlt = delta.reshape(lse.shape)
    stats = jnp.stack([lse, dlt])
    cut = (own - HALO) // LANES
    dm_l = lax.ppermute(dm_tail, AXES, up)
    dm_r = lax.ppermute(dm_head, AXES, down)
    st_l = lax.ppermute(stats[:, :, :, cut:], AXES, up)
    st_r = lax.ppermute(stats[:, :, :, : HALO // LANES], AXES, down)
    g_ff = lax.psum_scatter(g_ff, "fsdp", scatter_dimension=0, tiled=False)
    dq, dk, dv = attend_back_call(tab, q, k, v, d_mixed, lse, dlt, segc, segr)
    dk, dv = halo_back_call(tab, q, k, v, dm_l, dm_r, st_l, st_r, dk, dv, segc, segr)
    dlow, g_qv = low_back_call(dq, dv, tokens, sel, w_a, row(ln1_gain), row(ln1_bias))
    qv_grads = summed([g_qv[0], g_qv[1], g_qv[2], g_qv[3]], devices)
    narrow, deep = width // (devices // inner), b_up.shape[0] // (devices // inner)
    cuts = (0, narrow, 2 * narrow, 2 * narrow + deep, 2 * (narrow + deep))
    pieces = [g_ff[lo:hi].reshape(inner, -1, LANES) for lo, hi in zip(cuts[:-1], cuts[1:])]
    g_ff = jnp.concatenate(pieces, axis=1)
    if inner == 2:
        is_low = lax.axis_index("dp") == 0
        got = lax.ppermute(jnp.where(is_low, g_ff[1], g_ff[0]), "dp", [(0, 1), (1, 0)])
        mlp_grads = jnp.where(is_low, g_ff[0], g_ff[1]) + got
    else:
        mlp_grads = lax.psum_scatter(g_ff, "dp", scatter_dimension=0, tiled=False)
    grad_input = qkv_back_call(
        dq, dk, dv, dlow, tokens, d_resid, w_a, row(ln1_gain), row(ln1_bias)
    )
    return (
        block_out,
        grad_input,
        qv_grads[:r],
        qv_grads[r : 2 * r],
        qv_grads[2 * r : 3 * r],
        qv_grads[3 * r :],
        mlp_grads[:r],
        mlp_grads[2 * r : 2 * r + r_ff],
        mlp_grads[2 * r + r_ff :],
        mlp_grads[r : 2 * r],
    )


def solution(mesh):
    split = P(AXES, None)
    return jax.shard_map(
        local,
        mesh=mesh,
        in_specs=(
            split, split, P(), P(), P(), P(), split, P(), split, split, P(), split, P(), P(), P(),
            split, P(), split, P(), split, split, split, split, split, split, split, split,
        ),
        out_specs=(split,) * 10,
        check_vma=False,
    )
```

```python
import jax
import jax.numpy as jnp
from jax import lax
from jax.experimental import pallas as pl
from jax.experimental.pallas import tpu as pltpu
from jax.sharding import PartitionSpec as P


HEADS = 16
RANK = 16
ADAPTERS = 8
EPS = 1e-05
SLOPE = 1.702
NEG = -1000000000.0
AXES = ("fsdp", "dp")
LANES = 128
TILE = 256
HALO = 640
VMEM_LIMIT = 60 * 1024 * 1024
WIDE = 2

f32 = jnp.float32
bf16 = jnp.bfloat16


def dot_nn(a, b):
    return jnp.dot(a, b, preferred_element_type=f32)


def dot_nt(a, b):
    return lax.dot_general(a, b, (((1,), (1,)), ((), ())), preferred_element_type=f32)


def dot_tn(a, b):
    return lax.dot_general(a, b, (((0,), (0,)), ((), ())), preferred_element_type=f32)


def norm_forward(values, gain, shift):
    mean = jnp.mean(values, axis=1, keepdims=True)
    centered = values - mean
    inverse = lax.rsqrt(jnp.mean(centered * centered, axis=1, keepdims=True) + EPS)
    normed = centered * inverse
    return normed * gain + shift, normed, inverse


def norm_backward(grad, normed, inverse, gain):
    scaled = grad * gain
    return inverse * (
        scaled
        - jnp.mean(scaled, axis=1, keepdims=True)
        - normed * jnp.mean(scaled * normed, axis=1, keepdims=True)
    )


def params(grid_dims):
    return pltpu.CompilerParams(
        dimension_semantics=("arbitrary",) * grid_dims, vmem_limit_bytes=VMEM_LIMIT
    )


def whole(shape):
    return pl.BlockSpec(shape, lambda *_: (0,) * len(shape), pipeline_mode=pl.Buffered(1))


def twice(x):
    return jnp.concatenate([x, x], axis=1)


def qkv_kernel(tab, tok, sel, w, bq, bv, gain, shift, q_o, k_o, v_o):
    i = pl.program_id(0)
    needed = (i >= tab[12]) & (i <= tab[13])

    @pl.when(needed)
    def _():
        qkv_tile(tok, sel, w, bq, bv, gain, shift, q_o, k_o, v_o)

    @pl.when(jnp.logical_not(needed))
    def _():
        q_o[...] = jnp.zeros_like(q_o)
        k_o[...] = jnp.zeros_like(k_o)
        v_o[...] = jnp.zeros_like(v_o)


def qkv_tile(tok, sel, w, bq, bv, gain, shift, q_o, k_o, v_o):
    width = tok.shape[1]
    normal, _, _ = norm_forward(tok[...].astype(f32), gain[...], shift[...])
    n1 = normal.astype(bf16)
    select = sel[...]
    low = dot_nn(n1, w[:, 3 * width : 3 * width + 2 * LANES]).astype(bf16)
    low_q = low[:, :LANES] * select
    low_v = low[:, LANES:] * select
    q_out = w[:, 3 * width + 2 * LANES : 3 * width + 3 * LANES]
    v_out = w[:, 3 * width + 3 * LANES : 3 * width + 4 * LANES]
    scale = (width // HEADS) ** -0.5
    q = dot_nn(n1, w[:, :width]) + bq[...] + dot_nt(low_q, q_out)
    q_o[...] = (q * scale).astype(bf16)
    k_o[...] = dot_nn(n1, w[:, width : 2 * width]).astype(bf16)
    v = dot_nn(n1, w[:, 2 * width : 3 * width]) + bv[...] + dot_nt(low_v, v_out)
    v_o[...] = v.astype(bf16)


def qkv_call(tab, tok_w, sel_w, w_a, bq, bv, gain, shift):
    rows, width = tok_w.shape
    tile = pl.BlockSpec((TILE, width), lambda i, *_: (i, 0))
    vec = whole((1, width))
    out = jax.ShapeDtypeStruct((rows, width), bf16)
    return pl.pallas_call(
        qkv_kernel,
        grid_spec=pltpu.PrefetchScalarGridSpec(
            num_scalar_prefetch=1,
            grid=(rows // TILE,),
            in_specs=[
                tile,
                pl.BlockSpec((TILE, LANES), lambda i, *_: (i, 0)),
                whole((width, 3 * width + 4 * LANES)),
                vec,
                vec,
                vec,
                vec,
            ],
            out_specs=[tile] * 3,
        ),
        out_shape=[out] * 3,
        compiler_params=params(1),
        name="qkv",
    )(tab, tok_w, sel_w, w_a, bq, bv, gain, shift)


def head_masks(rows):
    lane = lax.broadcasted_iota(jnp.int32, (rows, LANES), 1)
    return lane < (LANES // 2)


def columns(c):
    return slice(c * LANES, (c + 1) * LANES)


def attend_kernel(tab, q, k, v, segc, segr, mixed_o, lse_o, s_scr):
    own = mixed_o.shape[0]
    wide = q.shape[1] // LANES
    first = head_masks(TILE)
    one = jnp.ones((), bf16)

    @pl.loop(0, own // TILE)
    def _(i):
        start, count = tab[2 * i], tab[2 * i + 1]
        row = pl.ds(pl.multiple_of(HALO + TILE * i, LANES), TILE)
        qs = [split_pair(q[row, columns(c)], first) for c in range(wide)]
        sq = twice(segc[row, :])

        def scores(t, carry):
            at = start + 2 * t
            here = pl.ds(pl.multiple_of(at * LANES, LANES), TILE)
            sk = jnp.concatenate([segr[pl.ds(at, 1), :], segr[pl.ds(at + 1, 1), :]], axis=1)
            mask = sq == sk
            out = []
            for c in range(wide):
                both = dot_nt(qs[c], k[here, columns(c)])
                for head in range(2):
                    x = jnp.where(mask, both[head * TILE : (head + 1) * TILE], NEG)
                    s_scr[2 * c + head, t] = x
                    out.append(
                        jnp.maximum(carry[2 * c + head], jnp.maximum(x[:, :LANES], x[:, LANES:]))
                    )
            return tuple(out)

        low = jnp.full((TILE, LANES), NEG, f32)
        tops = lax.fori_loop(0, count, scores, (low,) * (2 * wide))
        tops = [jnp.max(m, axis=1, keepdims=True) for m in tops]

        def weigh(t, carry):
            at = start + 2 * t
            here = pl.ds(pl.multiple_of(at * LANES, LANES), TILE)
            out = []
            for c in range(wide):
                vt = v[here, columns(c)]
                p0 = jnp.exp(s_scr[2 * c, t] - tops[2 * c]).astype(bf16)
                p1 = jnp.exp(s_scr[2 * c + 1, t] - tops[2 * c + 1]).astype(bf16)
                out.append(carry[2 * c] + dot_nn(p0, jnp.where(first, vt, one)))
                out.append(carry[2 * c + 1] + dot_nn(p1, jnp.where(first, one, vt)))
            return tuple(out)

        empty = jnp.zeros((TILE, LANES), f32)
        sums = lax.fori_loop(0, count, weigh, (empty,) * (2 * wide))
        for c in range(wide):
            a0, a1 = sums[2 * c], sums[2 * c + 1]
            r0 = pltpu.roll(a0, LANES // 2, 1)
            r1 = pltpu.roll(a1, LANES // 2, 1)
            out = jnp.where(first, a0 / r0, a1 / r1).astype(bf16)
            mixed_o[pl.ds(pl.multiple_of(TILE * i, TILE), TILE), columns(c)] = out
            l0 = (tops[2 * c] + jnp.log(jnp.where(first, r0, a0))).T
            l1 = (tops[2 * c + 1] + jnp.log(jnp.where(first, a1, r1))).T
            for half in range(2):
                at = 2 * i + half
                lse_o[c, 0, pl.ds(at, 1), :] = l0[0:1, columns(half)]
                lse_o[c, 1, pl.ds(at, 1), :] = l1[0:1, columns(half)]


def attend_call(tab, q, k, v, segc, segr, own):
    rows, width = q.shape
    pairs = width // LANES
    col = pl.BlockSpec((rows, WIDE * LANES), lambda h, *_: (0, h))
    return pl.pallas_call(
        attend_kernel,
        grid_spec=pltpu.PrefetchScalarGridSpec(
            num_scalar_prefetch=1,
            grid=(pairs // WIDE,),
            in_specs=[col, col, col, whole(segc.shape), whole(segr.shape)],
            out_specs=[
                pl.BlockSpec((own, WIDE * LANES), lambda h, *_: (0, h)),
                pl.BlockSpec((WIDE, 2, own // LANES, LANES), lambda h, *_: (h, 0, 0, 0)),
            ],
            scratch_shapes=[pltpu.VMEM((2 * WIDE, rows // TILE, TILE, TILE), f32)],
        ),
        out_shape=[
            jax.ShapeDtypeStruct((own, width), bf16),
            jax.ShapeDtypeStruct((pairs, 2, own // LANES, LANES), f32),
        ],
        compiler_params=params(1),
        name="attend",
    )(tab, q, k, v, segc, segr)


def split_pair(x, first):
    zero = jnp.zeros((), bf16)
    return jnp.concatenate([jnp.where(first, x, zero), jnp.where(first, zero, x)], axis=0)


def pair_grads(kt, vt, qcat, dcat, mask, lse0, lse1, dlt0, dlt1):
    half = qcat.shape[0] // 2
    s = dot_nt(kt, qcat)
    dp = dot_nt(vt, dcat)
    p0 = jnp.exp(jnp.where(mask, s[:, :half], NEG) - lse0)
    p1 = jnp.exp(jnp.where(mask, s[:, half:], NEG) - lse1)
    d0 = (p0 * (dp[:, :half] - dlt0)).astype(bf16)
    d1 = (p1 * (dp[:, half:] - dlt1)).astype(bf16)
    probs = jnp.concatenate([p0.astype(bf16), p1.astype(bf16)], axis=1)
    return probs, d0, d1


def attend_back_kernel(tab, q, k, v, dm, lse, dlt, segc, segr, dq_o, dk_o, dv_o, dk_a, dv_a):
    own = dm.shape[0]
    wide = q.shape[1] // LANES
    first = head_masks(TILE)
    scale = (LANES // 2) ** -0.5
    dk_a[...] = jnp.zeros_like(dk_a)
    dv_a[...] = jnp.zeros_like(dv_a)

    @pl.loop(0, own // TILE)
    def _(i):
        start, count = tab[2 * i], tab[2 * i + 1]
        row = pl.ds(pl.multiple_of(HALO + TILE * i, LANES), TILE)
        here = pl.ds(pl.multiple_of(TILE * i, TILE), TILE)
        qs = [split_pair(q[row, columns(c)], first) for c in range(wide)]
        ds = [split_pair(dm[here, columns(c)], first) for c in range(wide)]

        def line(ref, c, head):
            return jnp.concatenate(
                [ref[c, head, pl.ds(2 * i, 1), :], ref[c, head, pl.ds(2 * i + 1, 1), :]], axis=1
            )

        stats = [[line(ref, c, head) for ref in (lse, dlt) for head in range(2)] for c in range(wide)]
        at_q = HALO // LANES + 2 * i
        sq = jnp.concatenate([segr[pl.ds(at_q, 1), :], segr[pl.ds(at_q + 1, 1), :]], axis=1)

        def step(t, carry, size=TILE):
            at = pl.ds(pl.multiple_of((start + 2 * t) * LANES, LANES), size)
            mask = twice(segc[at, :]) == sq
            out = []
            for c in range(wide):
                kt = k[at, columns(c)]
                vt = v[at, columns(c)]
                probs, d0, d1 = pair_grads(kt, vt, qs[c], ds[c], mask, *stats[c])
                dv_a[at, columns(c)] += dot_nn(probs, ds[c])
                dk_a[at, columns(c)] += dot_nn(jnp.concatenate([d0, d1], axis=1), qs[c])
                out += [carry[2 * c] + dot_tn(d0, kt), carry[2 * c + 1] + dot_tn(d1, kt)]
            return tuple(out)

        empty = jnp.zeros((TILE, LANES), f32)
        sums = lax.fori_loop(
            0, count // 2, lambda t, c: step(2 * t, c, 2 * TILE), (empty,) * (2 * wide)
        )
        sums = lax.fori_loop(count // 2 * 2, count, step, sums)
        for c in range(wide):
            dq_o[here, columns(c)] = (
                jnp.where(first, sums[2 * c], sums[2 * c + 1]) * scale
            ).astype(bf16)

    dk_o[...] = dk_a[HALO : HALO + own, :]
    dv_o[...] = dv_a[HALO : HALO + own, :]


def attend_back_call(tab, q, k, v, dm, lse, dlt, segc, segr):
    rows, width = q.shape
    own = dm.shape[0]
    pairs = width // LANES
    col = pl.BlockSpec((rows, WIDE * LANES), lambda h, *_: (0, h))
    own_col = pl.BlockSpec((own, WIDE * LANES), lambda h, *_: (0, h))
    stat = pl.BlockSpec((WIDE, 2, own // LANES, LANES), lambda h, *_: (h, 0, 0, 0))
    return pl.pallas_call(
        attend_back_kernel,
        grid_spec=pltpu.PrefetchScalarGridSpec(
            num_scalar_prefetch=1,
            grid=(pairs // WIDE,),
            in_specs=[col, col, col, own_col, stat, stat, whole(segc.shape), whole(segr.shape)],
            out_specs=[own_col] * 3,
            scratch_shapes=[pltpu.VMEM((rows, WIDE * LANES), f32)] * 2,
        ),
        out_shape=[
            jax.ShapeDtypeStruct((own, width), bf16),
            jax.ShapeDtypeStruct((own, width), f32),
            jax.ShapeDtypeStruct((own, width), f32),
        ],
        compiler_params=params(1),
        name="attend_back",
    )(tab, q, k, v, dm, lse, dlt, segc, segr)


def halo_back_kernel(
    tab, q, k, v, dm_l, dm_r, st_l, st_r, dk_i, dv_i, segc, segr, dk_o, dv_o, dk_a, dv_a
):
    own = dk_o.shape[0]
    wide = q.shape[1] // LANES
    first = head_masks(LANES)
    dk_a[...] = dk_i[...]
    dv_a[...] = dv_i[...]
    for side in range(2):
        base = 6 + 3 * side
        count_q, k_first, count_k = tab[base], tab[base + 1], tab[base + 2]
        dm, st = (dm_l, st_l) if side == 0 else (dm_r, st_r)

        def query_tile(t, carry):
            tile = HALO // LANES - 1 - t if side == 0 else t
            tile_w = tile if side == 0 else tile + (HALO + own) // LANES
            at_h = pl.ds(pl.multiple_of(tile * LANES, LANES), LANES)
            at_w = pl.ds(pl.multiple_of(tile_w * LANES, LANES), LANES)
            qs = [split_pair(q[at_w, columns(c)], first) for c in range(wide)]
            ds = [split_pair(dm[at_h, columns(c)], first) for c in range(wide)]
            stats = [
                [st[kind, c, head, pl.ds(tile, 1), :] for kind in range(2) for head in range(2)]
                for c in range(wide)
            ]
            sq = segr[pl.ds(tile_w, 1), :]

            def key_tile(u, inner, size=TILE):
                at = pl.ds(pl.multiple_of((k_first + u) * TILE, TILE), size)
                at_k = pl.ds(pl.multiple_of(HALO + (k_first + u) * TILE, LANES), size)
                mask = segc[at_k, :] == sq
                for c in range(wide):
                    kt = k[at_k, columns(c)]
                    vt = v[at_k, columns(c)]
                    probs, d0, d1 = pair_grads(kt, vt, qs[c], ds[c], mask, *stats[c])
                    dv_a[at, columns(c)] += dot_nn(probs, ds[c])
                    dk_a[at, columns(c)] += dot_nn(jnp.concatenate([d0, d1], axis=1), qs[c])
                return inner

            carry = lax.fori_loop(
                0, count_k // 2, lambda u, c: key_tile(2 * u, c, 2 * TILE), carry
            )
            return lax.fori_loop(count_k // 2 * 2, count_k, key_tile, carry)

        lax.fori_loop(0, count_q, query_tile, 0)
    dk_o[...] = dk_a[...].astype(bf16)
    dv_o[...] = dv_a[...].astype(bf16)


def halo_back_call(tab, q, k, v, dm_l, dm_r, st_l, st_r, dk, dv, segc, segr):
    rows, width = q.shape
    own = dk.shape[0]
    pairs = width // LANES
    col = pl.BlockSpec((rows, WIDE * LANES), lambda h, *_: (0, h))
    own_col = pl.BlockSpec((own, WIDE * LANES), lambda h, *_: (0, h))
    halo_col = pl.BlockSpec((HALO, WIDE * LANES), lambda h, *_: (0, h))
    stat = pl.BlockSpec((2, WIDE, 2, HALO // LANES, LANES), lambda h, *_: (0, h, 0, 0, 0))
    return pl.pallas_call(
        halo_back_kernel,
        grid_spec=pltpu.PrefetchScalarGridSpec(
            num_scalar_prefetch=1,
            grid=(pairs // WIDE,),
            in_specs=[
                col,
                col,
                col,
                halo_col,
                halo_col,
                stat,
                stat,
                own_col,
                own_col,
                whole(segc.shape),
                whole(segr.shape),
            ],
            out_specs=[own_col] * 2,
            scratch_shapes=[pltpu.VMEM((own, WIDE * LANES), f32)] * 2,
        ),
        out_shape=[jax.ShapeDtypeStruct((own, width), bf16)] * 2,
        compiler_params=params(1),
        name="halo_back",
    )(tab, q, k, v, dm_l, dm_r, st_l, st_r, dk, dv, segc, segr)


FF_TILE = 512


def mlp_kernel(
    mixed, tok, dy, sel, w_out, w_up, w_lo, w_dn, w_x, b_out, b_up, b_down, gain, shift, heads,
    out_o, dres_o, dmix_o, head_o, tail_o, dlt_o, grads_o,
    resid, n2, low_u, dlow_d, low_ut, dlow_dt, acc, acc_low, dn2, dlow_u, gdo_t, gui_t,
):
    j = pl.program_id(0)
    rows, width = mixed.shape
    chunks = [pl.ds(r, TILE) for r in range(0, rows, TILE)]
    up_in = w_lo[:, :LANES]
    down_out = w_lo[:, LANES:]
    out_w = w_out[...].reshape(width, width)

    @pl.when(j == 0)
    def _():
        for r in chunks:
            x = tok[r, :].astype(f32) + dot_nn(mixed[r, :], out_w) + b_out[...]
            resid[r, :] = x
            normal, _, _ = norm_forward(x, gain[...], shift[...])
            normal = normal.astype(bf16)
            n2[r, :] = normal
            lu = dot_nn(normal, up_in).astype(bf16) * sel[r, :]
            ld = dot_nn(dy[r, :], down_out).astype(bf16) * sel[r, :]
            low_u[r, :] = lu
            dlow_d[r, :] = ld
            low_ut[:, r] = lu.astype(f32).T.astype(bf16)
            dlow_dt[:, r] = ld.astype(f32).T.astype(bf16)
        acc[...] = jnp.zeros_like(acc)
        acc_low[...] = jnp.zeros_like(acc_low)
        dn2[...] = jnp.zeros_like(dn2)
        dlow_u[...] = jnp.zeros_like(dlow_u)
        gdo_t[...] = jnp.zeros_like(gdo_t)
        gui_t[...] = jnp.zeros_like(gui_t)

    down = w_dn[...].reshape(FF_TILE, width)
    up_w = w_up[...].reshape(width, FF_TILE)
    if len(w_x.shape) == 2:
        up_out, down_in = w_x[:, :LANES], w_x[:, LANES:]
    else:
        x = w_x[...]
        columns = [slice(c, c + LANES) for c in range(0, width, LANES)]
        half = len(columns) // 2
        up_out = jnp.concatenate([x[p, :, c] for p in range(x.shape[0]) for c in columns[:half]], axis=0)
        down_in = jnp.concatenate([x[p, :, c] for p in range(x.shape[0]) for c in columns[half:]], axis=0)
    guo_t = jnp.zeros((LANES, FF_TILE), f32)
    gdi_t = jnp.zeros((LANES, FF_TILE), f32)
    for r in chunks:
        pre = dot_nn(n2[r, :], up_w) + b_up[...] + dot_nt(low_u[r, :], up_out)
        d_act = dot_nt(dy[r, :], down) + dot_nt(dlow_d[r, :], down_in)
        gate = 1.0 / (1.0 + jnp.exp(-SLOPE * pre))
        act = pre * gate
        d_pre = (d_act * (gate + SLOPE * act * (1.0 - gate))).astype(bf16)
        act = act.astype(bf16)
        acc[r, :] += dot_nn(act, down)
        acc_low[r, :] += dot_nn(act, down_in)
        dn2[r, :] += dot_nt(d_pre, up_w)
        dlow_u[r, :] += dot_nn(d_pre, up_out)
        guo_t += dot_nn(low_ut[:, r], d_pre)
        gdi_t += dot_nn(dlow_dt[:, r], act)
    owners, packed = grads_o.shape[:2]
    narrow = width // owners
    deep = packed // 2 - narrow
    group = FF_TILE // deep
    own_j = pl.ds(j * group, group)
    grads_o[own_j, 2 * narrow : 2 * narrow + deep, :] = guo_t.T.reshape(group, deep, LANES)
    grads_o[own_j, 2 * narrow + deep :, :] = gdi_t.T.reshape(group, deep, LANES)

    @pl.when(j == pl.num_programs(0) - 1)
    def _():
        for r in chunks:
            select = sel[r, :]
            x = resid[r, :]
            low_d = acc_low[r, :].astype(bf16) * select
            out_o[r, :] = (x + acc[r, :] + b_down[...] + dot_nt(low_d, down_out)).astype(bf16)
            lu = dlow_u[r, :].astype(bf16) * select
            _, hat, inv = norm_forward(x, gain[...], shift[...])
            grad = dn2[r, :] + dot_nt(lu, up_in)
            dres = dy[r, :].astype(f32) + norm_backward(grad, hat, inv, gain[...])
            dres_o[r, :] = dres
            dmix = dot_nt(dres.astype(bf16), out_w).astype(bf16)
            dmix_o[r, :] = dmix
            at = r.start
            upper = min(HALO - at, TILE)
            head_o[at : at + upper, :] = dmix[:upper]
            skip = max(rows - HALO - at, 0)
            first = at + skip - (rows - HALO)
            tail_o[first : first + TILE - skip, :] = dmix[skip:]
            prod = dmix.astype(f32) * mixed[r, :].astype(f32)
            high = prod.astype(bf16)
            rest = (prod - high.astype(f32)).astype(bf16)
            delta = dot_nt(heads[...], high) + dot_nt(heads[...], rest)
            for part in range(TILE // LANES):
                dlt_o[:, at // LANES + part, :] = delta[:, part * LANES : (part + 1) * LANES]
            gdo_t[...] += dot_nn(low_d.astype(f32).T.astype(bf16), dy[r, :])
            gui_t[...] += dot_nn(lu.astype(f32).T.astype(bf16), n2[r, :])
        grads_o[:, :narrow, :] = gui_t[...].T.reshape(owners, narrow, LANES)
        grads_o[:, narrow : 2 * narrow, :] = gdo_t[...].T.reshape(owners, narrow, LANES)


def mlp_call(mixed, tok, dy, sel, w_a, w_b, w_c, b_out, b_up, b_down, gain, shift, heads, owners):
    rows, width = mixed.shape
    hidden = b_up.shape[1]
    full = whole((rows, width))
    vec = whole((1, width))
    low = whole((rows, LANES))
    at_low = (3 * width + 4 * LANES) // (2 * LANES)
    packed = (owners, 2 * (width + hidden) // owners, LANES)
    const = lambda shape: pl.BlockSpec(shape, lambda j: (0,) * len(shape))
    once = pl.Buffered(1)
    if w_c is None:
        devices = w_b.shape[0]
        r, r_ff = width // devices, hidden // devices
        lead = (r_ff + r) // r
        per = width // FF_TILE
        at_x = lead + hidden // width
        group = FF_TILE // r_ff
        specs = [
            pl.BlockSpec((devices, r, width), lambda j: (0, r_ff // r, 0), pipeline_mode=once),
            pl.BlockSpec((devices, r, FF_TILE), lambda j: (0, lead + j // per, j % per)),
            pl.BlockSpec((group, r_ff, width), lambda j: (j, 0, 0)),
            pl.BlockSpec((group, r, width), lambda j: (j, at_x, 0)),
        ]
        weights = [w_b] * 4
    else:
        lead = width // FF_TILE
        specs = [
            whole((width, width)),
            pl.BlockSpec((width, FF_TILE), lambda j: (0, lead + j)),
            pl.BlockSpec((FF_TILE, width), lambda j: (j, 0)),
            pl.BlockSpec((FF_TILE, 2 * LANES), lambda j: (j, width // (2 * LANES))),
        ]
        weights = [w_b, w_b, w_c, w_c]
    return pl.pallas_call(
        mlp_kernel,
        grid=(hidden // FF_TILE,),
        in_specs=[
            full,
            full,
            full,
            low,
            specs[0],
            specs[1],
            pl.BlockSpec((width, 2 * LANES), lambda j: (0, at_low), pipeline_mode=once),
            specs[2],
            specs[3],
            vec,
            pl.BlockSpec((1, FF_TILE), lambda j: (0, j)),
            vec,
            vec,
            vec,
            whole(heads.shape),
        ],
        out_specs=[
            const((rows, width)),
            const((rows, width)),
            const((rows, width)),
            const((HALO, width)),
            const((HALO, width)),
            const((HEADS, rows // LANES, LANES)),
            const(packed),
        ],
        out_shape=[
            jax.ShapeDtypeStruct((rows, width), bf16),
            jax.ShapeDtypeStruct((rows, width), f32),
            jax.ShapeDtypeStruct((rows, width), bf16),
            jax.ShapeDtypeStruct((HALO, width), bf16),
            jax.ShapeDtypeStruct((HALO, width), bf16),
            jax.ShapeDtypeStruct((HEADS, rows // LANES, LANES), f32),
            jax.ShapeDtypeStruct(packed, f32),
        ],
        scratch_shapes=[
            pltpu.VMEM((rows, width), f32),
            pltpu.VMEM((rows, width), bf16),
            pltpu.VMEM((rows, LANES), bf16),
            pltpu.VMEM((rows, LANES), bf16),
            pltpu.VMEM((LANES, rows), bf16),
            pltpu.VMEM((LANES, rows), bf16),
            pltpu.VMEM((rows, width), f32),
            pltpu.VMEM((rows, LANES), f32),
            pltpu.VMEM((rows, width), f32),
            pltpu.VMEM((rows, LANES), f32),
            pltpu.VMEM((LANES, width), f32),
            pltpu.VMEM((LANES, width), f32),
        ],
        compiler_params=params(1),
        name="mlp",
    )(mixed, tok, dy, sel, weights[0], weights[1], w_a, weights[2], weights[3],
      b_out, b_up, b_down, gain, shift, heads)


def low_back_kernel(dq, dv, tok, sel, w, gain, shift, dlow_o, grads_o, acc):
    i = pl.program_id(0)
    normal, _, _ = norm_forward(tok[...].astype(f32), gain[...], shift[...])
    n1 = normal.astype(bf16)
    select = sel[...]
    low = dot_nn(n1, w[:, : 2 * LANES]).astype(bf16)
    low_q = low[:, :LANES] * select
    low_v = low[:, LANES:] * select
    dlow_q = dot_nn(dq[...], w[:, 2 * LANES : 3 * LANES]).astype(bf16) * select
    dlow_v = dot_nn(dv[...], w[:, 3 * LANES : 4 * LANES]).astype(bf16) * select
    dlow_o[:, :LANES] = dlow_q
    dlow_o[:, LANES:] = dlow_v

    @pl.when(i == 0)
    def _():
        acc[...] = jnp.zeros_like(acc)

    def turned(x):
        return x.astype(f32).T.astype(bf16)

    acc[0] += dot_nn(turned(dlow_q), n1)
    acc[1] += dot_nn(turned(low_q), dq[...])
    acc[2] += dot_nn(turned(dlow_v), n1)
    acc[3] += dot_nn(turned(low_v), dv[...])

    @pl.when(i == pl.num_programs(0) - 1)
    def _():
        for at in range(4):
            grads_o[at] = acc[at].T.astype(bf16)


def low_back_call(dq, dv, tok, sel, w_a, gain, shift):
    rows, width = tok.shape
    tile = pl.BlockSpec((TILE, width), lambda i: (i, 0))
    vec = whole((1, width))
    low = pl.BlockSpec((TILE, LANES), lambda i: (i, 0))
    at_low = 3 * width // (4 * LANES)
    return pl.pallas_call(
        low_back_kernel,
        grid=(rows // TILE,),
        in_specs=[
            tile,
            tile,
            tile,
            low,
            pl.BlockSpec((width, 4 * LANES), lambda i: (0, at_low), pipeline_mode=pl.Buffered(1)),
            vec,
            vec,
        ],
        out_specs=[
            pl.BlockSpec((TILE, 2 * LANES), lambda i: (i, 0)),
            pl.BlockSpec((4, width, LANES), lambda i: (0, 0, 0)),
        ],
        out_shape=[
            jax.ShapeDtypeStruct((rows, 2 * LANES), bf16),
            jax.ShapeDtypeStruct((4, width, LANES), bf16),
        ],
        scratch_shapes=[pltpu.VMEM((4, LANES, width), f32)],
        compiler_params=params(1),
        name="low_back",
    )(dq, dv, tok, sel, w_a, gain, shift)


def qkv_back_kernel(dq, dk, dv, dlow, tok, dres, w, gain, shift, gin_o):
    width = tok.shape[1]
    _, hat, inv = norm_forward(tok[...].astype(f32), gain[...], shift[...])
    grad = (
        dot_nt(dq[...], w[:, :width])
        + dot_nt(dk[...], w[:, width : 2 * width])
        + dot_nt(dv[...], w[:, 2 * width : 3 * width])
        + dot_nt(dlow[...], w[:, 3 * width : 3 * width + 2 * LANES])
    )
    gin_o[...] = (dres[...] + norm_backward(grad, hat, inv, gain[...])).astype(bf16)


def qkv_back_call(dq, dk, dv, dlow, tok, dres, w_a, gain, shift):
    rows, width = tok.shape
    tile = pl.BlockSpec((TILE, width), lambda i: (i, 0))
    vec = whole((1, width))
    return pl.pallas_call(
        qkv_back_kernel,
        grid=(rows // TILE,),
        in_specs=[
            tile,
            tile,
            tile,
            pl.BlockSpec((TILE, 2 * LANES), lambda i: (i, 0)),
            tile,
            tile,
            whole((width, 3 * width + 4 * LANES)),
            vec,
            vec,
        ],
        out_specs=tile,
        out_shape=jax.ShapeDtypeStruct((rows, width), bf16),
        compiler_params=params(1),
        name="qkv_back",
    )(dq, dk, dv, dlow, tok, dres, w_a, gain, shift)


def summed(parts, devices):
    packed = jnp.concatenate([p.reshape(devices, -1, p.shape[-1]) for p in parts], axis=1)
    got = lax.all_to_all(packed, AXES, 0, 0, tiled=True)
    return jnp.sum(got.astype(f32), axis=0)


def local(
    tokens, cotangent, segments, adapter_ids, ln1_gain, ln1_bias, w_query, b_query, w_key, w_value,
    b_value, w_out, b_out, ln2_gain, ln2_bias, w_up, b_up, w_down, b_down, query_in, query_out,
    value_in, value_out, up_in, up_out, down_in, down_out,
):
    own, width = tokens.shape
    inner = lax.axis_size("dp")
    devices = lax.axis_size("fsdp") * inner
    up = [(i, i + 1) for i in range(devices - 1)]
    down = [(i + 1, i) for i in range(devices - 1)]

    def gather(*pieces):
        return lax.all_gather(jnp.concatenate(pieces, axis=1), AXES, axis=0, tiled=True)

    before = lax.ppermute(tokens[own - HALO :], AXES, up)
    after = lax.ppermute(tokens[:HALO], AXES, down)
    first_maps = (w_query, w_key, w_value, query_in, value_in, query_out, value_out, up_in, down_out)
    r, r_ff = w_out.shape[0], w_down.shape[0]
    if inner == 2 and r % 16 == 0 and 2 * LANES * (r_ff // r) == width:
        chunks = [slice(c, c + r) for c in range(0, r_ff, r)]
        low_maps = jnp.concatenate([m[c] for m in (up_out, down_in) for c in chunks], axis=1)
        up_blocks = [w_up[:, c : c + width] for c in range(0, w_up.shape[1], width)]
        is_first = lax.axis_index("dp") == 0

        def gather_twice(mine):
            theirs = lax.ppermute(mine, "dp", [(0, 1), (1, 0)])
            both = jnp.stack([jnp.where(is_first, mine, theirs), jnp.where(is_first, theirs, mine)])
            return lax.all_gather(both, "fsdp", axis=0, tiled=True)

        w_a = gather_twice(jnp.concatenate(first_maps, axis=1)).reshape(r * devices, -1)
        w_b = gather_twice(jnp.concatenate([w_down, w_out, *up_blocks, low_maps], axis=0))
        w_c = None
    else:
        w_a = gather(*first_maps)
        w_b = gather(w_out, w_up)
        w_c = gather(w_down, up_out, down_in)

    position = lax.axis_index(AXES)
    padded = jnp.concatenate(
        [
            jnp.full((HALO,), -1, jnp.int32),
            segments,
            jnp.full((HALO,), 1 << 30, jnp.int32),
        ]
    )
    rows = own + 2 * HALO
    seg_w = lax.dynamic_slice_in_dim(padded, position * own, rows, 0)
    tile_seg = seg_w[HALO : HALO + own].reshape(own // TILE, TILE)
    images = jnp.concatenate([tile_seg[:, 0], tile_seg[:, -1]])
    low = jnp.sum((seg_w[None, :] < images[:, None]).astype(jnp.int32), axis=1)
    high = jnp.sum((seg_w[None, :] <= images[:, None]).astype(jnp.int32), axis=1)
    tiles = own // TILE
    entries = []
    for i in range(tiles):
        start = low[i] // LANES
        count = (high[tiles + i] - start * LANES + TILE - 1) // TILE
        entries += [jnp.minimum(start, rows // LANES - 2 * count), count]
    count_l = (HALO - low[0] + LANES - 1) // LANES
    entries += [
        jnp.maximum(count_l, 0),
        jnp.zeros((), jnp.int32),
        (jnp.minimum(high[0], HALO + own) - HALO + TILE - 1) // TILE,
    ]
    last = 2 * tiles - 1
    first_k = jnp.maximum(low[last] - HALO, 0) // TILE
    entries += [
        jnp.maximum((high[last] - HALO - own + LANES - 1) // LANES, 0),
        first_k,
        tiles - first_k,
        low[0] // TILE,
        (high[last] - 1) // TILE,
    ]
    tab = jnp.stack(entries)
    segr = seg_w.reshape(rows // LANES, LANES)
    segc = jnp.broadcast_to(seg_w[:, None], (rows, LANES))

    image_hot = (seg_w[:, None] == jnp.arange(adapter_ids.shape[0], dtype=jnp.int32)).astype(bf16)
    column = jnp.arange(ADAPTERS * RANK, dtype=jnp.int32) // RANK
    adapter_hot = (adapter_ids[:, None] == column[None, :]).astype(bf16)
    sel_w = dot_nn(image_hot, adapter_hot).astype(bf16)
    sel = sel_w[HALO : HALO + own]
    heads = (
        jnp.arange(width, dtype=jnp.int32)[None, :] // (width // HEADS)
        == jnp.arange(HEADS, dtype=jnp.int32)[:, None]
    ).astype(bf16)

    row = lambda x: x.reshape(1, -1)
    tok_w = jnp.concatenate([before, tokens, after], axis=0)
    q, k, v = qkv_call(
        tab, tok_w, sel_w, w_a, row(b_query), row(b_value), row(ln1_gain), row(ln1_bias)
    )
    mixed, lse = attend_call(tab, q, k, v, segc, segr, own)
    block_out, d_resid, d_mixed, dm_head, dm_tail, delta, g_ff = mlp_call(
        mixed, tokens, cotangent, sel, w_a, w_b, w_c, row(b_out), row(b_up), row(b_down),
        row(ln2_gain), row(ln2_bias), heads, devices // inner,
    )
    dlt = delta.reshape(lse.shape)
    stats = jnp.stack([lse, dlt])
    cut = (own - HALO) // LANES
    dm_l = lax.ppermute(dm_tail, AXES, up)
    dm_r = lax.ppermute(dm_head, AXES, down)
    st_l = lax.ppermute(stats[:, :, :, cut:], AXES, up)
    st_r = lax.ppermute(stats[:, :, :, : HALO // LANES], AXES, down)
    g_ff = lax.psum_scatter(g_ff, "fsdp", scatter_dimension=0, tiled=False)
    dq, dk, dv = attend_back_call(tab, q, k, v, d_mixed, lse, dlt, segc, segr)
    dk, dv = halo_back_call(tab, q, k, v, dm_l, dm_r, st_l, st_r, dk, dv, segc, segr)
    dlow, g_qv = low_back_call(dq, dv, tokens, sel, w_a, row(ln1_gain), row(ln1_bias))
    qv_grads = summed([g_qv[0], g_qv[1], g_qv[2], g_qv[3]], devices)
    narrow, deep = width // (devices // inner), b_up.shape[0] // (devices // inner)
    cuts = (0, narrow, 2 * narrow, 2 * narrow + deep, 2 * (narrow + deep))
    pieces = [g_ff[lo:hi].reshape(inner, -1, LANES) for lo, hi in zip(cuts[:-1], cuts[1:])]
    g_ff = jnp.concatenate(pieces, axis=1)
    if inner == 2:
        is_low = lax.axis_index("dp") == 0
        got = lax.ppermute(jnp.where(is_low, g_ff[1], g_ff[0]), "dp", [(0, 1), (1, 0)])
        mlp_grads = jnp.where(is_low, g_ff[0], g_ff[1]) + got
    else:
        mlp_grads = lax.psum_scatter(g_ff, "dp", scatter_dimension=0, tiled=False)
    grad_input = qkv_back_call(
        dq, dk, dv, dlow, tokens, d_resid, w_a, row(ln1_gain), row(ln1_bias)
    )
    return (
        block_out,
        grad_input,
        qv_grads[:r],
        qv_grads[r : 2 * r],
        qv_grads[2 * r : 3 * r],
        qv_grads[3 * r :],
        mlp_grads[:r],
        mlp_grads[2 * r : 2 * r + r_ff],
        mlp_grads[2 * r + r_ff :],
        mlp_grads[r : 2 * r],
    )


def solution(mesh):
    split = P(AXES, None)
    return jax.shard_map(
        local,
        mesh=mesh,
        in_specs=(
            split, split, P(), P(), P(), P(), split, P(), split, split, P(), split, P(), P(), P(),
            split, P(), split, P(), split, split, split, split, split, split, split, split,
        ),
        out_specs=(split,) * 10,
        check_vma=False,
    )
```

```python
import jax
import jax.numpy as jnp
from jax import lax
from jax.experimental import pallas as pl
from jax.experimental.pallas import tpu as pltpu
from jax.sharding import PartitionSpec as P


HEADS = 16
RANK = 16
ADAPTERS = 8
EPS = 1e-05
SLOPE = 1.702
NEG = -1000000000.0
AXES = ("fsdp", "dp")
LANES = 128
TILE = 256
HALO = 640
VMEM_LIMIT = 60 * 1024 * 1024
WIDE = 2

f32 = jnp.float32
bf16 = jnp.bfloat16


def dot_nn(a, b):
    return jnp.dot(a, b, preferred_element_type=f32)


def dot_nt(a, b):
    return lax.dot_general(a, b, (((1,), (1,)), ((), ())), preferred_element_type=f32)


def dot_tn(a, b):
    return lax.dot_general(a, b, (((0,), (0,)), ((), ())), preferred_element_type=f32)


def norm_forward(values, gain, shift):
    mean = jnp.mean(values, axis=1, keepdims=True)
    centered = values - mean
    inverse = lax.rsqrt(jnp.mean(centered * centered, axis=1, keepdims=True) + EPS)
    normed = centered * inverse
    return normed * gain + shift, normed, inverse


def norm_backward(grad, normed, inverse, gain):
    scaled = grad * gain
    return inverse * (
        scaled
        - jnp.mean(scaled, axis=1, keepdims=True)
        - normed * jnp.mean(scaled * normed, axis=1, keepdims=True)
    )


def params(grid_dims):
    return pltpu.CompilerParams(
        dimension_semantics=("arbitrary",) * grid_dims, vmem_limit_bytes=VMEM_LIMIT
    )


def whole(shape):
    return pl.BlockSpec(shape, lambda *_: (0,) * len(shape), pipeline_mode=pl.Buffered(1))


def twice(x):
    return jnp.concatenate([x, x], axis=1)


def qkv_kernel(tab, tok, sel, w, bq, bv, gain, shift, q_o, k_o, v_o):
    i = pl.program_id(0)
    needed = (i >= tab[12]) & (i <= tab[13])

    @pl.when(needed)
    def _():
        qkv_tile(tok, sel, w, bq, bv, gain, shift, q_o, k_o, v_o)

    @pl.when(jnp.logical_not(needed))
    def _():
        q_o[...] = jnp.zeros_like(q_o)
        k_o[...] = jnp.zeros_like(k_o)
        v_o[...] = jnp.zeros_like(v_o)


def qkv_tile(tok, sel, w, bq, bv, gain, shift, q_o, k_o, v_o):
    width = tok.shape[1]
    normal, _, _ = norm_forward(tok[...].astype(f32), gain[...], shift[...])
    n1 = normal.astype(bf16)
    select = sel[...]
    low = dot_nn(n1, w[:, 3 * width : 3 * width + 2 * LANES]).astype(bf16)
    low_q = low[:, :LANES] * select
    low_v = low[:, LANES:] * select
    q_out = w[:, 3 * width + 2 * LANES : 3 * width + 3 * LANES]
    v_out = w[:, 3 * width + 3 * LANES : 3 * width + 4 * LANES]
    scale = (width // HEADS) ** -0.5
    q = dot_nn(n1, w[:, :width]) + bq[...] + dot_nt(low_q, q_out)
    q_o[...] = (q * scale).astype(bf16)
    k_o[...] = dot_nn(n1, w[:, width : 2 * width]).astype(bf16)
    v = dot_nn(n1, w[:, 2 * width : 3 * width]) + bv[...] + dot_nt(low_v, v_out)
    v_o[...] = v.astype(bf16)


def qkv_call(tab, tok_w, sel_w, w_a, bq, bv, gain, shift):
    rows, width = tok_w.shape
    tile = pl.BlockSpec((TILE, width), lambda i, *_: (i, 0))
    vec = whole((1, width))
    out = jax.ShapeDtypeStruct((rows, width), bf16)
    return pl.pallas_call(
        qkv_kernel,
        grid_spec=pltpu.PrefetchScalarGridSpec(
            num_scalar_prefetch=1,
            grid=(rows // TILE,),
            in_specs=[
                tile,
                pl.BlockSpec((TILE, LANES), lambda i, *_: (i, 0)),
                whole((width, 3 * width + 4 * LANES)),
                vec,
                vec,
                vec,
                vec,
            ],
            out_specs=[tile] * 3,
        ),
        out_shape=[out] * 3,
        compiler_params=params(1),
        name="qkv",
    )(tab, tok_w, sel_w, w_a, bq, bv, gain, shift)


def head_masks(rows):
    lane = lax.broadcasted_iota(jnp.int32, (rows, LANES), 1)
    return lane < (LANES // 2)


def columns(c):
    return slice(c * LANES, (c + 1) * LANES)


def attend_kernel(tab, q, k, v, segc, segr, mixed_o, lse_o, s_scr):
    own = mixed_o.shape[0]
    wide = q.shape[1] // LANES
    first = head_masks(TILE)
    one = jnp.ones((), bf16)

    @pl.loop(0, own // TILE)
    def _(i):
        start, count = tab[2 * i], tab[2 * i + 1]
        row = pl.ds(pl.multiple_of(HALO + TILE * i, LANES), TILE)
        qs = [split_pair(q[row, columns(c)], first) for c in range(wide)]
        sq = twice(segc[row, :])

        def scores(t, carry):
            at = start + 2 * t
            here = pl.ds(pl.multiple_of(at * LANES, LANES), TILE)
            sk = jnp.concatenate([segr[pl.ds(at, 1), :], segr[pl.ds(at + 1, 1), :]], axis=1)
            mask = sq == sk
            out = []
            for c in range(wide):
                both = dot_nt(qs[c], k[here, columns(c)])
                for head in range(2):
                    x = jnp.where(mask, both[head * TILE : (head + 1) * TILE], NEG)
                    s_scr[2 * c + head, t] = x
                    out.append(
                        jnp.maximum(carry[2 * c + head], jnp.maximum(x[:, :LANES], x[:, LANES:]))
                    )
            return tuple(out)

        low = jnp.full((TILE, LANES), NEG, f32)
        tops = lax.fori_loop(0, count, scores, (low,) * (2 * wide))
        tops = [jnp.max(m, axis=1, keepdims=True) for m in tops]

        def weigh(t, carry):
            at = start + 2 * t
            here = pl.ds(pl.multiple_of(at * LANES, LANES), TILE)
            out = []
            for c in range(wide):
                vt = v[here, columns(c)]
                p0 = jnp.exp(s_scr[2 * c, t] - tops[2 * c]).astype(bf16)
                p1 = jnp.exp(s_scr[2 * c + 1, t] - tops[2 * c + 1]).astype(bf16)
                out.append(carry[2 * c] + dot_nn(p0, jnp.where(first, vt, one)))
                out.append(carry[2 * c + 1] + dot_nn(p1, jnp.where(first, one, vt)))
            return tuple(out)

        empty = jnp.zeros((TILE, LANES), f32)
        sums = lax.fori_loop(0, count, weigh, (empty,) * (2 * wide))
        for c in range(wide):
            a0, a1 = sums[2 * c], sums[2 * c + 1]
            r0 = pltpu.roll(a0, LANES // 2, 1)
            r1 = pltpu.roll(a1, LANES // 2, 1)
            out = jnp.where(first, a0 / r0, a1 / r1).astype(bf16)
            mixed_o[pl.ds(pl.multiple_of(TILE * i, TILE), TILE), columns(c)] = out
            l0 = (tops[2 * c] + jnp.log(jnp.where(first, r0, a0))).T
            l1 = (tops[2 * c + 1] + jnp.log(jnp.where(first, a1, r1))).T
            for half in range(2):
                at = 2 * i + half
                lse_o[c, 0, pl.ds(at, 1), :] = l0[0:1, columns(half)]
                lse_o[c, 1, pl.ds(at, 1), :] = l1[0:1, columns(half)]


def attend_call(tab, q, k, v, segc, segr, own):
    rows, width = q.shape
    pairs = width // LANES
    col = pl.BlockSpec((rows, WIDE * LANES), lambda h, *_: (0, h))
    return pl.pallas_call(
        attend_kernel,
        grid_spec=pltpu.PrefetchScalarGridSpec(
            num_scalar_prefetch=1,
            grid=(pairs // WIDE,),
            in_specs=[col, col, col, whole(segc.shape), whole(segr.shape)],
            out_specs=[
                pl.BlockSpec((own, WIDE * LANES), lambda h, *_: (0, h)),
                pl.BlockSpec((WIDE, 2, own // LANES, LANES), lambda h, *_: (h, 0, 0, 0)),
            ],
            scratch_shapes=[pltpu.VMEM((2 * WIDE, rows // TILE, TILE, TILE), f32)],
        ),
        out_shape=[
            jax.ShapeDtypeStruct((own, width), bf16),
            jax.ShapeDtypeStruct((pairs, 2, own // LANES, LANES), f32),
        ],
        compiler_params=params(1),
        name="attend",
    )(tab, q, k, v, segc, segr)


def split_pair(x, first):
    zero = jnp.zeros((), bf16)
    return jnp.concatenate([jnp.where(first, x, zero), jnp.where(first, zero, x)], axis=0)


def pair_grads(kt, vt, qcat, dcat, mask, lse0, lse1, dlt0, dlt1):
    half = qcat.shape[0] // 2
    s = dot_nt(kt, qcat)
    dp = dot_nt(vt, dcat)
    p0 = jnp.exp(jnp.where(mask, s[:, :half], NEG) - lse0)
    p1 = jnp.exp(jnp.where(mask, s[:, half:], NEG) - lse1)
    d0 = (p0 * (dp[:, :half] - dlt0)).astype(bf16)
    d1 = (p1 * (dp[:, half:] - dlt1)).astype(bf16)
    probs = jnp.concatenate([p0.astype(bf16), p1.astype(bf16)], axis=1)
    return probs, d0, d1


def attend_back_kernel(tab, q, k, v, dm, lse, dlt, segc, segr, dq_o, dk_o, dv_o, dk_a, dv_a):
    own = dm.shape[0]
    wide = q.shape[1] // LANES
    first = head_masks(TILE)
    scale = (LANES // 2) ** -0.5
    dk_a[...] = jnp.zeros_like(dk_a)
    dv_a[...] = jnp.zeros_like(dv_a)

    @pl.loop(0, own // TILE)
    def _(i):
        start, count = tab[2 * i], tab[2 * i + 1]
        row = pl.ds(pl.multiple_of(HALO + TILE * i, LANES), TILE)
        here = pl.ds(pl.multiple_of(TILE * i, TILE), TILE)
        qs = [split_pair(q[row, columns(c)], first) for c in range(wide)]
        ds = [split_pair(dm[here, columns(c)], first) for c in range(wide)]

        def line(ref, c, head):
            return jnp.concatenate(
                [ref[c, head, pl.ds(2 * i, 1), :], ref[c, head, pl.ds(2 * i + 1, 1), :]], axis=1
            )

        stats = [[line(ref, c, head) for ref in (lse, dlt) for head in range(2)] for c in range(wide)]
        at_q = HALO // LANES + 2 * i
        sq = jnp.concatenate([segr[pl.ds(at_q, 1), :], segr[pl.ds(at_q + 1, 1), :]], axis=1)

        def step(t, carry, size=TILE):
            at = pl.ds(pl.multiple_of((start + 2 * t) * LANES, LANES), size)
            mask = twice(segc[at, :]) == sq
            out = []
            for c in range(wide):
                kt = k[at, columns(c)]
                vt = v[at, columns(c)]
                probs, d0, d1 = pair_grads(kt, vt, qs[c], ds[c], mask, *stats[c])
                dv_a[at, columns(c)] += dot_nn(probs, ds[c])
                dk_a[at, columns(c)] += dot_nn(jnp.concatenate([d0, d1], axis=1), qs[c])
                out += [carry[2 * c] + dot_tn(d0, kt), carry[2 * c + 1] + dot_tn(d1, kt)]
            return tuple(out)

        empty = jnp.zeros((TILE, LANES), f32)
        sums = lax.fori_loop(
            0, count // 2, lambda t, c: step(2 * t, c, 2 * TILE), (empty,) * (2 * wide)
        )
        sums = lax.fori_loop(count // 2 * 2, count, step, sums)
        for c in range(wide):
            dq_o[here, columns(c)] = (
                jnp.where(first, sums[2 * c], sums[2 * c + 1]) * scale
            ).astype(bf16)

    dk_o[...] = dk_a[HALO : HALO + own, :]
    dv_o[...] = dv_a[HALO : HALO + own, :]


def attend_back_call(tab, q, k, v, dm, lse, dlt, segc, segr):
    rows, width = q.shape
    own = dm.shape[0]
    pairs = width // LANES
    col = pl.BlockSpec((rows, WIDE * LANES), lambda h, *_: (0, h))
    own_col = pl.BlockSpec((own, WIDE * LANES), lambda h, *_: (0, h))
    stat = pl.BlockSpec((WIDE, 2, own // LANES, LANES), lambda h, *_: (h, 0, 0, 0))
    return pl.pallas_call(
        attend_back_kernel,
        grid_spec=pltpu.PrefetchScalarGridSpec(
            num_scalar_prefetch=1,
            grid=(pairs // WIDE,),
            in_specs=[col, col, col, own_col, stat, stat, whole(segc.shape), whole(segr.shape)],
            out_specs=[own_col] * 3,
            scratch_shapes=[pltpu.VMEM((rows, WIDE * LANES), f32)] * 2,
        ),
        out_shape=[
            jax.ShapeDtypeStruct((own, width), bf16),
            jax.ShapeDtypeStruct((own, width), f32),
            jax.ShapeDtypeStruct((own, width), f32),
        ],
        compiler_params=params(1),
        name="attend_back",
    )(tab, q, k, v, dm, lse, dlt, segc, segr)


def halo_back_kernel(
    tab, q, k, v, dm_l, dm_r, st_l, st_r, dk_i, dv_i, segc, segr, dk_o, dv_o, dk_a, dv_a
):
    own = dk_o.shape[0]
    wide = q.shape[1] // LANES
    first = head_masks(LANES)
    dk_a[...] = dk_i[...]
    dv_a[...] = dv_i[...]
    for side in range(2):
        base = 6 + 3 * side
        count_q, k_first, count_k = tab[base], tab[base + 1], tab[base + 2]
        dm, st = (dm_l, st_l) if side == 0 else (dm_r, st_r)

        def query_tile(t, carry):
            tile = HALO // LANES - 1 - t if side == 0 else t
            tile_w = tile if side == 0 else tile + (HALO + own) // LANES
            at_h = pl.ds(pl.multiple_of(tile * LANES, LANES), LANES)
            at_w = pl.ds(pl.multiple_of(tile_w * LANES, LANES), LANES)
            qs = [split_pair(q[at_w, columns(c)], first) for c in range(wide)]
            ds = [split_pair(dm[at_h, columns(c)], first) for c in range(wide)]
            stats = [
                [st[kind, c, head, pl.ds(tile, 1), :] for kind in range(2) for head in range(2)]
                for c in range(wide)
            ]
            sq = segr[pl.ds(tile_w, 1), :]

            def key_tile(u, inner, size=TILE):
                at = pl.ds(pl.multiple_of((k_first + u) * TILE, TILE), size)
                at_k = pl.ds(pl.multiple_of(HALO + (k_first + u) * TILE, LANES), size)
                mask = segc[at_k, :] == sq
                for c in range(wide):
                    kt = k[at_k, columns(c)]
                    vt = v[at_k, columns(c)]
                    probs, d0, d1 = pair_grads(kt, vt, qs[c], ds[c], mask, *stats[c])
                    dv_a[at, columns(c)] += dot_nn(probs, ds[c])
                    dk_a[at, columns(c)] += dot_nn(jnp.concatenate([d0, d1], axis=1), qs[c])
                return inner

            carry = lax.fori_loop(
                0, count_k // 2, lambda u, c: key_tile(2 * u, c, 2 * TILE), carry
            )
            return lax.fori_loop(count_k // 2 * 2, count_k, key_tile, carry)

        lax.fori_loop(0, count_q, query_tile, 0)
    dk_o[...] = dk_a[...].astype(bf16)
    dv_o[...] = dv_a[...].astype(bf16)


def halo_back_call(tab, q, k, v, dm_l, dm_r, st_l, st_r, dk, dv, segc, segr):
    rows, width = q.shape
    own = dk.shape[0]
    pairs = width // LANES
    col = pl.BlockSpec((rows, WIDE * LANES), lambda h, *_: (0, h))
    own_col = pl.BlockSpec((own, WIDE * LANES), lambda h, *_: (0, h))
    halo_col = pl.BlockSpec((HALO, WIDE * LANES), lambda h, *_: (0, h))
    stat = pl.BlockSpec((2, WIDE, 2, HALO // LANES, LANES), lambda h, *_: (0, h, 0, 0, 0))
    return pl.pallas_call(
        halo_back_kernel,
        grid_spec=pltpu.PrefetchScalarGridSpec(
            num_scalar_prefetch=1,
            grid=(pairs // WIDE,),
            in_specs=[
                col,
                col,
                col,
                halo_col,
                halo_col,
                stat,
                stat,
                own_col,
                own_col,
                whole(segc.shape),
                whole(segr.shape),
            ],
            out_specs=[own_col] * 2,
            scratch_shapes=[pltpu.VMEM((own, WIDE * LANES), f32)] * 2,
        ),
        out_shape=[jax.ShapeDtypeStruct((own, width), bf16)] * 2,
        compiler_params=params(1),
        name="halo_back",
    )(tab, q, k, v, dm_l, dm_r, st_l, st_r, dk, dv, segc, segr)


FF_TILE = 512
FF_ROWS = 768


def mlp_kernel(
    mixed, tok, dy, sel, w_out, w_up, w_lo, w_dn, w_x, b_out, b_up, b_down, gain, shift, heads,
    out_o, dres_o, dmix_o, head_o, tail_o, dlt_o, grads_o,
    resid, n2, low_u, dlow_d, low_ut, dlow_dt, acc, acc_low, dn2, dlow_u, gdo_t, gui_t,
):
    j = pl.program_id(0)
    rows, width = mixed.shape
    chunks = [pl.ds(r, FF_ROWS) for r in range(0, rows, FF_ROWS)]
    up_in = w_lo[:, :LANES]
    down_out = w_lo[:, LANES:]
    out_w = w_out[...].reshape(width, width)

    @pl.when(j == 0)
    def _():
        for r in chunks:
            x = tok[r, :].astype(f32) + dot_nn(mixed[r, :], out_w) + b_out[...]
            resid[r, :] = x
            normal, _, _ = norm_forward(x, gain[...], shift[...])
            normal = normal.astype(bf16)
            n2[r, :] = normal
            lu = dot_nn(normal, up_in).astype(bf16) * sel[r, :]
            ld = dot_nn(dy[r, :], down_out).astype(bf16) * sel[r, :]
            low_u[r, :] = lu
            dlow_d[r, :] = ld
            low_ut[:, r] = lu.astype(f32).T.astype(bf16)
            dlow_dt[:, r] = ld.astype(f32).T.astype(bf16)
        acc[...] = jnp.zeros_like(acc)
        acc_low[...] = jnp.zeros_like(acc_low)
        dn2[...] = jnp.zeros_like(dn2)
        dlow_u[...] = jnp.zeros_like(dlow_u)
        gdo_t[...] = jnp.zeros_like(gdo_t)
        gui_t[...] = jnp.zeros_like(gui_t)

    down = w_dn[...].reshape(FF_TILE, width)
    up_w = w_up[...].reshape(width, FF_TILE)
    if len(w_x.shape) == 2:
        up_out, down_in = w_x[:, :LANES], w_x[:, LANES:]
    else:
        x = w_x[...]
        columns = [slice(c, c + LANES) for c in range(0, width, LANES)]
        half = len(columns) // 2
        up_out = jnp.concatenate([x[p, :, c] for p in range(x.shape[0]) for c in columns[:half]], axis=0)
        down_in = jnp.concatenate([x[p, :, c] for p in range(x.shape[0]) for c in columns[half:]], axis=0)
    guo_t = jnp.zeros((LANES, FF_TILE), f32)
    gdi_t = jnp.zeros((LANES, FF_TILE), f32)
    for r in chunks:
        pre = dot_nn(n2[r, :], up_w) + b_up[...] + dot_nt(low_u[r, :], up_out)
        d_act = dot_nt(dy[r, :], down) + dot_nt(dlow_d[r, :], down_in)
        gate = 1.0 / (1.0 + jnp.exp(-SLOPE * pre))
        act = pre * gate
        d_pre = (d_act * (gate + SLOPE * act * (1.0 - gate))).astype(bf16)
        act = act.astype(bf16)
        acc[r, :] += dot_nn(act, down)
        acc_low[r, :] += dot_nn(act, down_in)
        dn2[r, :] += dot_nt(d_pre, up_w)
        dlow_u[r, :] += dot_nn(d_pre, up_out)
        guo_t += dot_nn(low_ut[:, r], d_pre)
        gdi_t += dot_nn(dlow_dt[:, r], act)
    owners, packed = grads_o.shape[:2]
    narrow = width // owners
    deep = packed // 2 - narrow
    group = FF_TILE // deep
    own_j = pl.ds(j * group, group)
    grads_o[own_j, 2 * narrow : 2 * narrow + deep, :] = guo_t.T.reshape(group, deep, LANES)
    grads_o[own_j, 2 * narrow + deep :, :] = gdi_t.T.reshape(group, deep, LANES)

    @pl.when(j == pl.num_programs(0) - 1)
    def _():
        for r in chunks:
            select = sel[r, :]
            x = resid[r, :]
            low_d = acc_low[r, :].astype(bf16) * select
            out_o[r, :] = (x + acc[r, :] + b_down[...] + dot_nt(low_d, down_out)).astype(bf16)
            lu = dlow_u[r, :].astype(bf16) * select
            _, hat, inv = norm_forward(x, gain[...], shift[...])
            grad = dn2[r, :] + dot_nt(lu, up_in)
            dres = dy[r, :].astype(f32) + norm_backward(grad, hat, inv, gain[...])
            dres_o[r, :] = dres
            dmix = dot_nt(dres.astype(bf16), out_w).astype(bf16)
            dmix_o[r, :] = dmix
            at = r.start
            upper = min(HALO - at, FF_ROWS)
            head_o[at : at + upper, :] = dmix[:upper]
            skip = max(rows - HALO - at, 0)
            first = at + skip - (rows - HALO)
            tail_o[first : first + FF_ROWS - skip, :] = dmix[skip:]
            prod = dmix.astype(f32) * mixed[r, :].astype(f32)
            high = prod.astype(bf16)
            rest = (prod - high.astype(f32)).astype(bf16)
            delta = dot_nt(heads[...], high) + dot_nt(heads[...], rest)
            for part in range(FF_ROWS // LANES):
                dlt_o[:, at // LANES + part, :] = delta[:, part * LANES : (part + 1) * LANES]
            gdo_t[...] += dot_nn(low_d.astype(f32).T.astype(bf16), dy[r, :])
            gui_t[...] += dot_nn(lu.astype(f32).T.astype(bf16), n2[r, :])
        grads_o[:, :narrow, :] = gui_t[...].T.reshape(owners, narrow, LANES)
        grads_o[:, narrow : 2 * narrow, :] = gdo_t[...].T.reshape(owners, narrow, LANES)


def mlp_call(mixed, tok, dy, sel, w_a, w_b, w_c, b_out, b_up, b_down, gain, shift, heads, owners):
    rows, width = mixed.shape
    hidden = b_up.shape[1]
    full = whole((rows, width))
    vec = whole((1, width))
    low = whole((rows, LANES))
    at_low = (3 * width + 4 * LANES) // (2 * LANES)
    packed = (owners, 2 * (width + hidden) // owners, LANES)
    const = lambda shape: pl.BlockSpec(shape, lambda j: (0,) * len(shape))
    once = pl.Buffered(1)
    if w_c is None:
        devices = w_b.shape[0]
        r, r_ff = width // devices, hidden // devices
        lead = (r_ff + r) // r
        per = width // FF_TILE
        at_x = lead + hidden // width
        group = FF_TILE // r_ff
        specs = [
            pl.BlockSpec((devices, r, width), lambda j: (0, r_ff // r, 0), pipeline_mode=once),
            pl.BlockSpec((devices, r, FF_TILE), lambda j: (0, lead + j // per, j % per)),
            pl.BlockSpec((group, r_ff, width), lambda j: (j, 0, 0)),
            pl.BlockSpec((group, r, width), lambda j: (j, at_x, 0)),
        ]
        weights = [w_b] * 4
    else:
        lead = width // FF_TILE
        specs = [
            whole((width, width)),
            pl.BlockSpec((width, FF_TILE), lambda j: (0, lead + j)),
            pl.BlockSpec((FF_TILE, width), lambda j: (j, 0)),
            pl.BlockSpec((FF_TILE, 2 * LANES), lambda j: (j, width // (2 * LANES))),
        ]
        weights = [w_b, w_b, w_c, w_c]
    return pl.pallas_call(
        mlp_kernel,
        grid=(hidden // FF_TILE,),
        in_specs=[
            full,
            full,
            full,
            low,
            specs[0],
            specs[1],
            pl.BlockSpec((width, 2 * LANES), lambda j: (0, at_low), pipeline_mode=once),
            specs[2],
            specs[3],
            vec,
            pl.BlockSpec((1, FF_TILE), lambda j: (0, j)),
            vec,
            vec,
            vec,
            whole(heads.shape),
        ],
        out_specs=[
            const((rows, width)),
            const((rows, width)),
            const((rows, width)),
            const((HALO, width)),
            const((HALO, width)),
            const((HEADS, rows // LANES, LANES)),
            const(packed),
        ],
        out_shape=[
            jax.ShapeDtypeStruct((rows, width), bf16),
            jax.ShapeDtypeStruct((rows, width), f32),
            jax.ShapeDtypeStruct((rows, width), bf16),
            jax.ShapeDtypeStruct((HALO, width), bf16),
            jax.ShapeDtypeStruct((HALO, width), bf16),
            jax.ShapeDtypeStruct((HEADS, rows // LANES, LANES), f32),
            jax.ShapeDtypeStruct(packed, f32),
        ],
        scratch_shapes=[
            pltpu.VMEM((rows, width), f32),
            pltpu.VMEM((rows, width), bf16),
            pltpu.VMEM((rows, LANES), bf16),
            pltpu.VMEM((rows, LANES), bf16),
            pltpu.VMEM((LANES, rows), bf16),
            pltpu.VMEM((LANES, rows), bf16),
            pltpu.VMEM((rows, width), f32),
            pltpu.VMEM((rows, LANES), f32),
            pltpu.VMEM((rows, width), f32),
            pltpu.VMEM((rows, LANES), f32),
            pltpu.VMEM((LANES, width), f32),
            pltpu.VMEM((LANES, width), f32),
        ],
        compiler_params=params(1),
        name="mlp",
    )(mixed, tok, dy, sel, weights[0], weights[1], w_a, weights[2], weights[3],
      b_out, b_up, b_down, gain, shift, heads)


def low_back_kernel(dq, dv, tok, sel, w, gain, shift, dlow_o, grads_o, acc):
    i = pl.program_id(0)
    normal, _, _ = norm_forward(tok[...].astype(f32), gain[...], shift[...])
    n1 = normal.astype(bf16)
    select = sel[...]
    low = dot_nn(n1, w[:, : 2 * LANES]).astype(bf16)
    low_q = low[:, :LANES] * select
    low_v = low[:, LANES:] * select
    dlow_q = dot_nn(dq[...], w[:, 2 * LANES : 3 * LANES]).astype(bf16) * select
    dlow_v = dot_nn(dv[...], w[:, 3 * LANES : 4 * LANES]).astype(bf16) * select
    dlow_o[:, :LANES] = dlow_q
    dlow_o[:, LANES:] = dlow_v

    @pl.when(i == 0)
    def _():
        acc[...] = jnp.zeros_like(acc)

    def turned(x):
        return x.astype(f32).T.astype(bf16)

    acc[0] += dot_nn(turned(dlow_q), n1)
    acc[1] += dot_nn(turned(low_q), dq[...])
    acc[2] += dot_nn(turned(dlow_v), n1)
    acc[3] += dot_nn(turned(low_v), dv[...])

    @pl.when(i == pl.num_programs(0) - 1)
    def _():
        for at in range(4):
            grads_o[at] = acc[at].T.astype(bf16)


def low_back_call(dq, dv, tok, sel, w_a, gain, shift):
    rows, width = tok.shape
    tile = pl.BlockSpec((TILE, width), lambda i: (i, 0))
    vec = whole((1, width))
    low = pl.BlockSpec((TILE, LANES), lambda i: (i, 0))
    at_low = 3 * width // (4 * LANES)
    return pl.pallas_call(
        low_back_kernel,
        grid=(rows // TILE,),
        in_specs=[
            tile,
            tile,
            tile,
            low,
            pl.BlockSpec((width, 4 * LANES), lambda i: (0, at_low), pipeline_mode=pl.Buffered(1)),
            vec,
            vec,
        ],
        out_specs=[
            pl.BlockSpec((TILE, 2 * LANES), lambda i: (i, 0)),
            pl.BlockSpec((4, width, LANES), lambda i: (0, 0, 0)),
        ],
        out_shape=[
            jax.ShapeDtypeStruct((rows, 2 * LANES), bf16),
            jax.ShapeDtypeStruct((4, width, LANES), bf16),
        ],
        scratch_shapes=[pltpu.VMEM((4, LANES, width), f32)],
        compiler_params=params(1),
        name="low_back",
    )(dq, dv, tok, sel, w_a, gain, shift)


def qkv_back_kernel(dq, dk, dv, dlow, tok, dres, w, gain, shift, gin_o):
    width = tok.shape[1]
    _, hat, inv = norm_forward(tok[...].astype(f32), gain[...], shift[...])
    grad = (
        dot_nt(dq[...], w[:, :width])
        + dot_nt(dk[...], w[:, width : 2 * width])
        + dot_nt(dv[...], w[:, 2 * width : 3 * width])
        + dot_nt(dlow[...], w[:, 3 * width : 3 * width + 2 * LANES])
    )
    gin_o[...] = (dres[...] + norm_backward(grad, hat, inv, gain[...])).astype(bf16)


def qkv_back_call(dq, dk, dv, dlow, tok, dres, w_a, gain, shift):
    rows, width = tok.shape
    tile = pl.BlockSpec((TILE, width), lambda i: (i, 0))
    vec = whole((1, width))
    return pl.pallas_call(
        qkv_back_kernel,
        grid=(rows // TILE,),
        in_specs=[
            tile,
            tile,
            tile,
            pl.BlockSpec((TILE, 2 * LANES), lambda i: (i, 0)),
            tile,
            tile,
            whole((width, 3 * width + 4 * LANES)),
            vec,
            vec,
        ],
        out_specs=tile,
        out_shape=jax.ShapeDtypeStruct((rows, width), bf16),
        compiler_params=params(1),
        name="qkv_back",
    )(dq, dk, dv, dlow, tok, dres, w_a, gain, shift)


def summed(parts, devices):
    packed = jnp.concatenate([p.reshape(devices, -1, p.shape[-1]) for p in parts], axis=1)
    got = lax.all_to_all(packed, AXES, 0, 0, tiled=True)
    return jnp.sum(got.astype(f32), axis=0)


def local(
    tokens, cotangent, segments, adapter_ids, ln1_gain, ln1_bias, w_query, b_query, w_key, w_value,
    b_value, w_out, b_out, ln2_gain, ln2_bias, w_up, b_up, w_down, b_down, query_in, query_out,
    value_in, value_out, up_in, up_out, down_in, down_out,
):
    own, width = tokens.shape
    inner = lax.axis_size("dp")
    devices = lax.axis_size("fsdp") * inner
    up = [(i, i + 1) for i in range(devices - 1)]
    down = [(i + 1, i) for i in range(devices - 1)]

    def gather(*pieces):
        return lax.all_gather(jnp.concatenate(pieces, axis=1), AXES, axis=0, tiled=True)

    before = lax.ppermute(tokens[own - HALO :], AXES, up)
    after = lax.ppermute(tokens[:HALO], AXES, down)
    first_maps = (w_query, w_key, w_value, query_in, value_in, query_out, value_out, up_in, down_out)
    r, r_ff = w_out.shape[0], w_down.shape[0]
    if inner == 2 and r % 16 == 0 and 2 * LANES * (r_ff // r) == width:
        chunks = [slice(c, c + r) for c in range(0, r_ff, r)]
        low_maps = jnp.concatenate([m[c] for m in (up_out, down_in) for c in chunks], axis=1)
        up_blocks = [w_up[:, c : c + width] for c in range(0, w_up.shape[1], width)]
        is_first = lax.axis_index("dp") == 0

        def gather_twice(mine):
            theirs = lax.ppermute(mine, "dp", [(0, 1), (1, 0)])
            both = jnp.stack([jnp.where(is_first, mine, theirs), jnp.where(is_first, theirs, mine)])
            return lax.all_gather(both, "fsdp", axis=0, tiled=True)

        w_a = gather_twice(jnp.concatenate(first_maps, axis=1)).reshape(r * devices, -1)
        w_b = gather_twice(jnp.concatenate([w_down, w_out, *up_blocks, low_maps], axis=0))
        w_c = None
    else:
        w_a = gather(*first_maps)
        w_b = gather(w_out, w_up)
        w_c = gather(w_down, up_out, down_in)

    position = lax.axis_index(AXES)
    padded = jnp.concatenate(
        [
            jnp.full((HALO,), -1, jnp.int32),
            segments,
            jnp.full((HALO,), 1 << 30, jnp.int32),
        ]
    )
    rows = own + 2 * HALO
    seg_w = lax.dynamic_slice_in_dim(padded, position * own, rows, 0)
    tile_seg = seg_w[HALO : HALO + own].reshape(own // TILE, TILE)
    images = jnp.concatenate([tile_seg[:, 0], tile_seg[:, -1]])
    low = jnp.sum((seg_w[None, :] < images[:, None]).astype(jnp.int32), axis=1)
    high = jnp.sum((seg_w[None, :] <= images[:, None]).astype(jnp.int32), axis=1)
    tiles = own // TILE
    entries = []
    for i in range(tiles):
        start = low[i] // LANES
        count = (high[tiles + i] - start * LANES + TILE - 1) // TILE
        entries += [jnp.minimum(start, rows // LANES - 2 * count), count]
    count_l = (HALO - low[0] + LANES - 1) // LANES
    entries += [
        jnp.maximum(count_l, 0),
        jnp.zeros((), jnp.int32),
        (jnp.minimum(high[0], HALO + own) - HALO + TILE - 1) // TILE,
    ]
    last = 2 * tiles - 1
    first_k = jnp.maximum(low[last] - HALO, 0) // TILE
    entries += [
        jnp.maximum((high[last] - HALO - own + LANES - 1) // LANES, 0),
        first_k,
        tiles - first_k,
        low[0] // TILE,
        (high[last] - 1) // TILE,
    ]
    tab = jnp.stack(entries)
    segr = seg_w.reshape(rows // LANES, LANES)
    segc = jnp.broadcast_to(seg_w[:, None], (rows, LANES))

    image_hot = (seg_w[:, None] == jnp.arange(adapter_ids.shape[0], dtype=jnp.int32)).astype(bf16)
    column = jnp.arange(ADAPTERS * RANK, dtype=jnp.int32) // RANK
    adapter_hot = (adapter_ids[:, None] == column[None, :]).astype(bf16)
    sel_w = dot_nn(image_hot, adapter_hot).astype(bf16)
    sel = sel_w[HALO : HALO + own]
    heads = (
        jnp.arange(width, dtype=jnp.int32)[None, :] // (width // HEADS)
        == jnp.arange(HEADS, dtype=jnp.int32)[:, None]
    ).astype(bf16)

    row = lambda x: x.reshape(1, -1)
    tok_w = jnp.concatenate([before, tokens, after], axis=0)
    q, k, v = qkv_call(
        tab, tok_w, sel_w, w_a, row(b_query), row(b_value), row(ln1_gain), row(ln1_bias)
    )
    mixed, lse = attend_call(tab, q, k, v, segc, segr, own)
    block_out, d_resid, d_mixed, dm_head, dm_tail, delta, g_ff = mlp_call(
        mixed, tokens, cotangent, sel, w_a, w_b, w_c, row(b_out), row(b_up), row(b_down),
        row(ln2_gain), row(ln2_bias), heads, devices // inner,
    )
    dlt = delta.reshape(lse.shape)
    stats = jnp.stack([lse, dlt])
    cut = (own - HALO) // LANES
    dm_l = lax.ppermute(dm_tail, AXES, up)
    dm_r = lax.ppermute(dm_head, AXES, down)
    st_l = lax.ppermute(stats[:, :, :, cut:], AXES, up)
    st_r = lax.ppermute(stats[:, :, :, : HALO // LANES], AXES, down)
    g_ff = lax.psum_scatter(g_ff, "fsdp", scatter_dimension=0, tiled=False)
    dq, dk, dv = attend_back_call(tab, q, k, v, d_mixed, lse, dlt, segc, segr)
    dk, dv = halo_back_call(tab, q, k, v, dm_l, dm_r, st_l, st_r, dk, dv, segc, segr)
    dlow, g_qv = low_back_call(dq, dv, tokens, sel, w_a, row(ln1_gain), row(ln1_bias))
    qv_grads = summed([g_qv[0], g_qv[1], g_qv[2], g_qv[3]], devices)
    narrow, deep = width // (devices // inner), b_up.shape[0] // (devices // inner)
    cuts = (0, narrow, 2 * narrow, 2 * narrow + deep, 2 * (narrow + deep))
    pieces = [g_ff[lo:hi].reshape(inner, -1, LANES) for lo, hi in zip(cuts[:-1], cuts[1:])]
    g_ff = jnp.concatenate(pieces, axis=1)
    if inner == 2:
        is_low = lax.axis_index("dp") == 0
        got = lax.ppermute(jnp.where(is_low, g_ff[1], g_ff[0]), "dp", [(0, 1), (1, 0)])
        mlp_grads = jnp.where(is_low, g_ff[0], g_ff[1]) + got
    else:
        mlp_grads = lax.psum_scatter(g_ff, "dp", scatter_dimension=0, tiled=False)
    grad_input = qkv_back_call(
        dq, dk, dv, dlow, tokens, d_resid, w_a, row(ln1_gain), row(ln1_bias)
    )
    return (
        block_out,
        grad_input,
        qv_grads[:r],
        qv_grads[r : 2 * r],
        qv_grads[2 * r : 3 * r],
        qv_grads[3 * r :],
        mlp_grads[:r],
        mlp_grads[2 * r : 2 * r + r_ff],
        mlp_grads[2 * r + r_ff :],
        mlp_grads[r : 2 * r],
    )


def solution(mesh):
    split = P(AXES, None)
    return jax.shard_map(
        local,
        mesh=mesh,
        in_specs=(
            split, split, P(), P(), P(), P(), split, P(), split, split, P(), split, P(), P(), P(),
            split, P(), split, P(), split, split, split, split, split, split, split, split,
        ),
        out_specs=(split,) * 10,
        check_vma=False,
    )
```
